256 devices in a mesh: row: 16 (over y_hi, x, core), col: 16 (over y_lo, z).
Axes of the slice: x: 4, y: 4 (y_hi: 2, y_lo: 2; y = y_hi * 2 + y_lo), z: 8, core: 2. Of those that a mesh axis runs over, the one named last changes fastest.
Arguments:
- op_tiles: float32 [512, 16, 64, 64], P('row', 'col'), may hold values from -18 to 18
- op_rows: int32 [512, 16], P('row', 'col'), may hold values from 0 to 7
- op_cols: int32 [512, 16], P('row', 'col'), may hold values from 0 to 7
- op_count: int32 [16, 16], P('row', 'col'), may hold values from 1 to 32, as said below
- pro_tiles: float32 [128, 16, 64, 64], P('row', 'col'), may hold values from -0.125 to 0.125
- pro_cols: int32 [128, 16], P('row', 'col'), may hold values from 0 to 1
- pro_live: int32 [128, 16], P('row', 'col'), may hold values 0 or 1
Outputs:
- product: float32 [128, 32, 64, 64], P('row', 'col')
- coarse: float32 [32, 32, 64, 64], P('row', 'col')
The draws below stay inside these ranges and needn't reach their ends.
Inputs may be any that keep to these rules, and one draw needn't show every extreme that they name: `op_count`: live slots of each device's list; some device's list is full in every draw.
All inputs are finite; a program needn't handle non-finite values. No bound on the sum of `pro_live` on one device may be relied on, other than what follows from the above.
Results may differ from the reference program's by a relative error of at most 0.0003.
Values sent between devices are 32-bit elements; how exact they have to be, the bound alone decides.
A program may use at most 128 MiB of HBM per device.

```python
import jax
import jax.numpy as jnp
from jax import lax

TILE = 64
FR = 8
LA = 32
NF = 128
FC = 8
NC = 32
NCC = 2
N_ROW = 16
N_COL = 16


def draw_op_count(key, part):
    base_key, heavy_key, chosen_key = jax.random.split(key, 3)
    light_counts = jax.random.randint(base_key, (N_ROW, N_COL), 1, LA // 2 + 1)
    heavy_marks = jax.random.randint(heavy_key, (N_ROW, N_COL), 0, 8) == 0
    counts = jnp.where(heavy_marks, LA, light_counts).reshape(-1)
    chosen_slot = jax.random.randint(chosen_key, (), 0, N_ROW * N_COL)
    flat_counts = jnp.where(jnp.arange(N_ROW * N_COL) == chosen_slot, LA, counts)
    return flat_counts.reshape(N_ROW, N_COL).astype(jnp.int32)


def touch_ends(entries, own_key, low, top_value):
    longest = entries.shape.index(max(entries.shape))
    spots = []
    for shift in (0, 1):
        where = [jax.random.randint(jax.random.fold_in(own_key, axis), (), 0, length) for axis, length in enumerate(entries.shape)]
        where[longest] = (where[longest] + shift) % entries.shape[longest]
        spots.append(tuple(where))
    return entries.at[spots[0]].set(low).at[spots[1]].set(top_value)


def block_levels(key, extent, cuts, smallest, largest):
    factor_of, own = 1.0, jax.random.fold_in(key, 6)
    for axis_at, blocks in cuts:
        steps = jnp.exp(jax.random.uniform(jax.random.fold_in(own, axis_at), (blocks,), jnp.float32, smallest / len(cuts), largest / len(cuts)))
        factor_of = factor_of * jnp.repeat(steps, extent[axis_at] // blocks).reshape([-1 if axis == axis_at else 1 for axis in range(len(extent))])
    return factor_of


def scatter_about(stream_key, shape, scale, bound, cuts=(), held_as=jnp.bfloat16):
    values = scale * jax.random.normal(stream_key, shape, jnp.float32)
    if cuts:
        values = values * block_levels(stream_key, shape, cuts, -0.22, 0.18)
    return jnp.clip(values, -bound, bound).astype(held_as)


def setup_inputs(seed: int = 0) -> dict:
    keys = jax.random.split(jax.random.key(seed), 8)
    op_tiles = scatter_about(keys[0], (N_ROW * LA, N_COL, TILE, TILE), 3.0, 18.0, ((0, 16), (1, 16)), jnp.float32)
    op_rows = touch_ends(jax.random.randint(keys[1], (N_ROW * LA, N_COL), 0, FR), jax.random.fold_in(keys[1], 1), 0, FR - 1).astype(jnp.int32)
    op_cols = touch_ends(jax.random.randint(keys[2], (N_ROW * LA, N_COL), 0, FC), jax.random.fold_in(keys[2], 1), 0, FC - 1).astype(jnp.int32)
    op_count = draw_op_count(jax.random.fold_in(keys[7], 71), 0)
    pro_tiles = scatter_about(keys[4], (NF, N_COL, TILE, TILE), (TILE * NF // 4) ** -0.5, 0.125, ((0, 16), (1, 16)), jnp.float32)
    pro_cols = touch_ends(jax.random.randint(keys[5], (NF, N_COL), 0, NCC), jax.random.fold_in(keys[5], 1), 0, NCC - 1).astype(jnp.int32)
    pro_live = touch_ends((jax.random.randint(keys[6], (NF, N_COL), 0, 2) < 1).astype(jnp.int32), jax.random.fold_in(keys[6], 1), 0, 1)
    return {"op_tiles": op_tiles, "op_rows": op_rows, "op_cols": op_cols, "op_count": op_count, "pro_tiles": pro_tiles, "pro_cols": pro_cols, "pro_live": pro_live}


precise = lax.Precision.HIGHEST


def reference(op_tiles, op_rows, op_cols, op_count, pro_tiles, pro_cols, pro_live):
    slot_ids = jnp.arange(LA, dtype=jnp.int32)
    live_op = (slot_ids[None, :, None] < op_count[:, None, :]).astype(jnp.float32)
    row_base = (jnp.arange(N_ROW, dtype=jnp.int32) * FR)[:, None, None]
    col_base = (jnp.arange(N_COL, dtype=jnp.int32) * FC)[None, None, :]
    glob_rows = (op_rows.reshape(N_ROW, LA, N_COL) + row_base).reshape(-1).astype(jnp.int32)
    glob_cols = (op_cols.reshape(N_ROW, LA, N_COL) + col_base).reshape(-1).astype(jnp.int32)
    masked_op = (op_tiles.reshape(N_ROW, LA, N_COL, TILE, TILE) * live_op[..., None, None]).reshape(-1, TILE, TILE)
    masked_pro = pro_tiles * pro_live.astype(jnp.float32)[..., None, None]
    coarse_ids = (pro_cols + (jnp.arange(N_COL, dtype=jnp.int32) * NCC)[None, :]).astype(jnp.int32)
    per_block = LA * N_COL

    def add_block(product_acc, block_id):
        begin_at = (block_id * per_block).astype(jnp.int32)
        tiles_blk = lax.dynamic_slice_in_dim(masked_op, begin_at, per_block, 0)
        rows_blk = lax.dynamic_slice_in_dim(glob_rows, begin_at, per_block, 0)
        cols_blk = lax.dynamic_slice_in_dim(glob_cols, begin_at, per_block, 0)
        right_tiles = masked_pro[cols_blk]
        targets = coarse_ids[cols_blk]
        tile_prods = jnp.einsum("nab,nsbc->nsac", tiles_blk, right_tiles, precision=precise)
        return product_acc.at[rows_blk[:, None], targets].add(tile_prods), None

    product = jnp.zeros((NF, NC, TILE, TILE), jnp.float32)
    product, unused_a = lax.scan(add_block, product, jnp.arange(N_ROW, dtype=jnp.int32))

    def add_coarse(coarse_acc, block_id):
        begin_at = (block_id * FR).astype(jnp.int32)
        left_tiles = lax.dynamic_slice_in_dim(masked_pro, begin_at, FR, 0)
        left_ids = lax.dynamic_slice_in_dim(coarse_ids, begin_at, FR, 0)
        right_rows = lax.dynamic_slice_in_dim(product, begin_at, FR, 0)
        tile_prods = jnp.einsum("ksba,kjbc->ksjac", left_tiles, right_rows, precision=precise)
        return coarse_acc.at[left_ids.reshape(-1)].add(tile_prods.reshape(-1, NC, TILE, TILE)), None

    coarse = jnp.zeros((NC, NC, TILE, TILE), jnp.float32)
    coarse, unused_b = lax.scan(add_coarse, coarse, jnp.arange(N_ROW, dtype=jnp.int32))
    return (product, coarse)
```

```python
import functools

import jax
import jax.numpy as jnp
from jax import lax
from jax.experimental import pallas as pl
from jax.experimental.pallas import tpu as pltpu
from jax.sharding import PartitionSpec as P

MESH = pl.DeviceIdType.MESH
F32, BF16 = jnp.float32, jnp.bfloat16
UR = 264
UH = 136
LA = 32
HALF = ((0, 256), (256, 256))

A_ID, T_ID, Y_ID = 0, 1, 2
X_ID = 3
CORE_ID = 11
Z_ID = 19
PY_ID = 27
RS_ID = 35
CC_ID = 51
CX_ID = 53
CY_ID = 57
N_ID = 58


def split(v):
    hi = v.astype(BF16)
    return hi, (v - hi.astype(F32)).astype(BF16)


def pack(tile):
    return jnp.concatenate([tile[:32], tile[32:]], axis=1)


def kernel(
    op_ref, rows_ref, cols_ref, count_ref, pro_ref, pcols_ref, plive_ref,
    prod_ref, coarse_ref,
    unit, alist, anear, panel, pror, ahi, alo, rhi, rlo, q, rsr, rsl, pthi, ptlo, phi, plo,
    cpart, crecv, xr0, xl0, xr1, xl1, yrecv,
    ssem, rsem, lsem,
):
    r = lax.axis_index("row")
    c = lax.axis_index("col")
    yh, x, core = r // 8, lax.rem(r // 2, 4), lax.rem(r, 2)
    yl, z = c // 8, lax.rem(c, 8)

    def rowdev(yh_, x_, core_):
        return ((yh_ * 4 + x_) * 2 + core_, c)

    ynear = (r, (1 - yl) * 8 + z)
    zright, zleft = (r, yl * 8 + lax.rem(z + 1, 8)), (r, yl * 8 + lax.rem(z + 7, 8))
    xright, xleft = rowdev(yh, lax.rem(x + 1, 4), core), rowdev(yh, lax.rem(x + 3, 4), core)
    yfar = rowdev(1 - yh, x, core)
    other = rowdev(yh, x, 1 - core)
    s0 = 2 * x + core
    across = ((yh * 4 + z // 2) * 2 + lax.rem(z, 2), yl * 8 + s0)
    own_across = s0 == z

    def send(src, dst, k, dev):
        pltpu.make_async_remote_copy(
            src_ref=src, dst_ref=dst, send_sem=ssem.at[k], recv_sem=rsem.at[k], device_id=dev, device_id_type=MESH
        ).start()

    def arrived(dst, k):
        pltpu.make_async_remote_copy(
            src_ref=dst, dst_ref=dst, send_sem=ssem.at[k], recv_sem=rsem.at[k], device_id=ynear, device_id_type=MESH
        ).wait_recv()

    def sent(src, k):
        pltpu.make_async_remote_copy(
            src_ref=src, dst_ref=src, send_sem=ssem.at[k], recv_sem=rsem.at[k], device_id=ynear, device_id_type=MESH
        ).wait_send()

    barrier = pltpu.get_barrier_semaphore()
    for dev in (ynear, zright, zleft, xright, xleft, yfar, other):
        pl.semaphore_signal(barrier, inc=1, device_id=dev, device_id_type=MESH)

    @pl.when(jnp.logical_not(own_across))
    def _():
        pl.semaphore_signal(barrier, inc=1, device_id=across, device_id_type=MESH)

    for k in range(8):
        live = plive_ref[k, 0].astype(F32)
        unit[pl.ds(k * 32, 32), :] = pack(pro_ref[k]) * live
        unit[pl.ds(256 + k, 1), :] = jnp.full((1, 128), pcols_ref[k, 0].astype(F32))

    pl.semaphore_wait(barrier, jnp.where(own_across, 7, 8))

    @pl.when(own_across)
    def _():
        pltpu.make_async_copy(unit, panel.at[yh, z], lsem.at[0]).start()

    @pl.when(jnp.logical_not(own_across))
    def _():
        send(unit, panel.at[yh, z], T_ID, across)

    keep = pltpu.make_async_copy(unit, pror.at[yl, z], lsem.at[1])
    keep.start()

    def pack_slot(t, carry):
        alist[t] = pack(op_ref[t])
        pos = jnp.where(t < count_ref[0, 0], rows_ref[t, 0] * 8 + cols_ref[t, 0], -1)
        alist[LA, pl.ds(t, 1), :] = jnp.full((1, 128), pos.astype(F32))
        return carry

    lax.fori_loop(0, LA, pack_slot, 0)
    send(alist, anear, A_ID, ynear)

    left32 = lax.broadcasted_iota(jnp.int32, (32, 128), 1) < 64

    def build_a(src, at):
        def row(i, carry):
            base = (i * 8).astype(F32)

            def slot(t, accs):
                tile = src[t]
                pos = src[LA, pl.ds(t, 1), :]
                return tuple(
                    acc + jnp.where(jnp.broadcast_to(pos == base + float(k), (32, 128)), tile, 0.0)
                    for k, acc in enumerate(accs)
                )

            accs = lax.fori_loop(0, LA, slot, tuple(jnp.zeros((32, 128), F32) for _ in range(8)))
            for m in range(4):
                even, odd = accs[2 * m], accs[2 * m + 1]
                top = jnp.where(left32, even, pltpu.roll(odd, 64, 1))
                bot = jnp.where(left32, pltpu.roll(even, 64, 1), odd)
                for off, v in ((0, top), (32, bot)):
                    hi, lo = split(v)
                    at_rows = pl.ds(pl.multiple_of(i * 64 + off, 32), 32)
                    ahi[at, at_rows, pl.ds(m * 128, 128)] = hi
                    alo[at, at_rows, pl.ds(m * 128, 128)] = lo
            return carry

        lax.fori_loop(0, 8, row, 0)

    build_a(alist, yl)

    def dense(ref, b, s, k):
        tile = ref[b, s, pl.ds(k * 32, 32), :]
        col = ref[b, s, pl.ds(256 + k, 1), :]
        turned = pltpu.roll(tile, 64, 1)
        a, bb = 1.0 - col, col
        top = jnp.where(left32, tile * a, turned * bb)
        bot = jnp.where(left32, turned * a, tile * bb)
        return top, bot

    @pl.when(own_across)
    def _():
        pltpu.make_async_copy(unit, panel.at[yh, z], lsem.at[0]).wait()

    @pl.when(jnp.logical_not(own_across))
    def _():
        arrived(panel.at[yh, s0], T_ID)

    sl, sr = lax.rem(s0 + 6, 8), lax.rem(s0 + 2, 8)
    sf = lax.rem(s0 + 4, 8)
    lo_half, hi_half = pl.ds(0, UH), pl.ds(UH, UR - UH)

    def spread(b, k):
        u = panel.at[b, s0]
        send(u, u, k, xright)
        send(u, u, k + 1, xleft)

    mine, theirs = yh, 1 - yh
    u = panel.at[mine, s0]
    send(u, u, Y_ID, yfar)
    spread(mine, X_ID)
    send(u, u, CORE_ID, other)
    keep.wait()
    zu = pror.at[yl, z]
    send(zu, zu, Z_ID, zright)
    send(zu, zu, Z_ID + 4, zleft)
    send(zu, zu, PY_ID, ynear)

    def pass_on(b, k, kc):
        u = panel.at[b, sl]
        arrived(u, k)
        send(u.at[lo_half], u.at[lo_half], k + 2, xright)
        send(u, u, kc, other)
        u = panel.at[b, sr]
        arrived(u, k + 1)
        send(u.at[hi_half], u.at[hi_half], k + 3, xleft)
        send(u, u, kc + 1, other)

    def zstep(step):
        got_r = pror.at[yl, lax.rem(z + 8 - step, 8)]
        got_l = pror.at[yl, lax.rem(z + step, 8)]
        arrived(got_r, Z_ID + step - 1)
        arrived(got_l, Z_ID + 4 + step - 1)
        if step < 3:
            send(got_r, got_r, Z_ID + step, zright)
            send(got_l, got_l, Z_ID + 4 + step, zleft)
        else:
            send(got_r.at[lo_half], got_r.at[lo_half], Z_ID + 3, zright)
            send(got_l.at[hi_half], got_l.at[hi_half], Z_ID + 7, zleft)
        send(got_r, got_r, PY_ID + 2 * step - 1, ynear)
        send(got_l, got_l, PY_ID + 2 * step, ynear)

    pass_on(mine, X_ID, CORE_ID + 1)
    u = panel.at[theirs, s0]
    arrived(u, Y_ID)
    spread(theirs, X_ID + 4)
    send(u, u, CORE_ID + 4, other)
    zstep(1)
    far = panel.at[mine, sf]
    arrived(far.at[lo_half], X_ID + 2)
    arrived(far.at[hi_half], X_ID + 3)
    send(far, far, CORE_ID + 3, other)
    pass_on(theirs, X_ID + 4, CORE_ID + 5)
    zstep(2)
    arrived(anear, A_ID)
    build_a(anear, 1 - yl)
    far2 = panel.at[theirs, sf]
    arrived(far2.at[lo_half], X_ID + 6)
    arrived(far2.at[hi_half], X_ID + 7)
    send(far2, far2, CORE_ID + 7, other)
    zstep(3)
    o0 = 2 * x + 1 - core
    from_other = [
        panel.at[b, lax.rem(o0 + off, 8)] for b in (mine, theirs) for off in (0, 6, 2, 4)
    ]
    for n, ref in enumerate(from_other):
        arrived(ref, CORE_ID + n)

    def build_r(d, at):
        s = lax.rem(z + d, 8)

        def block(b, carry):
            for k in range(8):
                for off, v in zip((0, 32), dense(panel, b, s, k)):
                    hi, lo = split(v)
                    rhi[b, pl.ds(k * 64 + off, 32), pl.ds(at * 128, 128)] = hi
                    rlo[b, pl.ds(k * 64 + off, 32), pl.ds(at * 128, 128)] = lo
            return carry

        lax.fori_loop(0, 2, block, 0)

    def dot(a, b):
        return lax.dot_general(a, b, (((1,), (0,)), ((), ())), preferred_element_type=F32)

    def chunk(d0, d1):
        build_r(d0, 0)
        build_r(d1, 1)

        def part(m, carry):
            rows = pl.ds(pl.multiple_of(m * 256, 256), 256)
            acc = jnp.zeros((256, 256), F32)
            for b in range(2):
                h, l = ahi[b, rows, :], alo[b, rows, :]
                acc = acc + dot(h, rhi[b]) + dot(h, rlo[b]) + dot(l, rhi[b])
            q[d0, rows, :] = acc[:, :128]
            q[d1, rows, :] = acc[:, 128:]
            return carry

        lax.fori_loop(0, 2, part, 0)

    def rs_id(step, half, way):
        return RS_ID + (step * 2 + half) * 2 + way

    def rs_send(d, step, half, way):
        rows = pl.ds(*HALF[half])
        buf = (rsr, rsl)[way]
        send(q.at[d, rows], buf.at[step, rows], rs_id(step, half, way), (zright, zleft)[way])

    def rs_add(d, step, half, way):
        rows = pl.ds(*HALF[half])
        buf = (rsr, rsl)[way]
        arrived(buf.at[step, rows], rs_id(step, half, way))
        q[d, rows, :] = q[d, rows, :] + buf[step, rows, :]

    def build_t(b, s):
        for m in range(4):
            t0, b0 = dense(pror, b, s, 2 * m)
            t1, b1 = dense(pror, b, s, 2 * m + 1)
            v = jnp.concatenate([t0, b0, t1, b1], axis=0).T
            hi, lo = split(v)
            pthi[b * 8 + s, :, pl.ds(m * 128, 128)] = hi
            ptlo[b * 8 + s, :, pl.ds(m * 128, 128)] = lo

    chunk(4, 0)
    rs_send(4, 0, 0, 0)
    rs_send(4, 0, 1, 1)
    chunk(3, 5)
    rs_send(3, 1, 1, 0)
    rs_send(5, 1, 0, 1)
    rs_add(3, 0, 0, 0)
    rs_send(3, 1, 0, 0)
    rs_add(5, 0, 1, 1)
    rs_send(5, 1, 1, 1)
    chunk(2, 6)

    zfar = pror.at[yl, lax.rem(z + 4, 8)]
    arrived(zfar.at[lo_half], Z_ID + 3)
    arrived(zfar.at[hi_half], Z_ID + 7)
    send(zfar, zfar, PY_ID + 7, ynear)

    for half_r, half_l in ((1, 0), (0, 1)):
        rs_add(2, 1, half_r, 0)
        rs_send(2, 2, half_r, 0)
        rs_add(6, 1, half_l, 1)
        rs_send(6, 2, half_l, 1)
    chunk(1, 7)

    def own_t(s, carry):
        build_t(yl, s)
        return carry

    for half_r, half_l in ((1, 0), (0, 1)):
        rs_add(1, 2, half_r, 0)
        rs_send(1, 3, half_r, 0)
        rs_add(7, 2, half_l, 1)
        rs_send(7, 3, half_l, 1)
    lax.fori_loop(0, 8, own_t, 0)

    near = [pror.at[1 - yl, z]]
    for step in (1, 2, 3):
        near += [pror.at[1 - yl, lax.rem(z + 8 - step, 8)], pror.at[1 - yl, lax.rem(z + step, 8)]]
    near.append(pror.at[1 - yl, lax.rem(z + 4, 8)])
    for n, ref in enumerate(near):
        arrived(ref, PY_ID + n)

    def near_t(s, carry):
        build_t(1 - yl, s)
        return carry

    lax.fori_loop(0, 8, near_t, 0)

    for half in (0, 1):
        rs_add(0, 3, half, 0)
        rs_add(0, 3, half, 1)
        rows = pl.ds(*HALF[half])
        hi, lo = split(q[0, rows, :])
        phi[rows, :] = hi
        plo[rows, :] = lo

    def coarse_part(gc):
        def one(g, carry):
            at = g * 2 + gc
            h, l = pthi[at], ptlo[at]
            v = dot(h, phi[...]) + dot(h, plo[...]) + dot(l, phi[...])
            cpart[gc, lax.rem(g, 4), g // 4] = v
            return carry

        lax.fori_loop(0, 8, one, 0)

    coarse_part(1 - core)
    send(cpart.at[1 - core], crecv, CC_ID, other)
    coarse_part(core)
    for i in range(8):
        v = q[0, pl.ds(i * 64, 64), :]
        prod_ref[i, 0] = v[:, :64]
        prod_ref[i, 1] = v[:, 64:]
    arrived(crecv, CC_ID)

    def add_core(n, carry):
        cpart[core, n] = cpart[core, n] + crecv[n]
        return carry

    x2 = lax.rem(x + 2, 4)
    xp, xm = lax.rem(x + 1, 4), lax.rem(x + 3, 4)
    cp = cpart.at[core]
    add_core(x2, 0)
    send(cp.at[x2, 0], xr0, CX_ID, xright)
    send(cp.at[x2, 1], xl0, CX_ID + 1, xleft)
    add_core(xp, 0)
    add_core(xm, 0)
    add_core(x, 0)
    arrived(xr0, CX_ID)
    cpart[core, xp, 0] = cpart[core, xp, 0] + xr0[...]
    send(cp.at[xp], xr1, CX_ID + 2, xright)
    arrived(xl0, CX_ID + 1)
    cpart[core, xm, 1] = cpart[core, xm, 1] + xl0[...]
    send(cp.at[xm], xl1, CX_ID + 3, xleft)
    arrived(xr1, CX_ID + 2)
    arrived(xl1, CX_ID + 3)
    cpart[core, x, 1 - yh] = cpart[core, x, 1 - yh] + xr1[1 - yh] + xl1[1 - yh]
    send(cp.at[x, 1 - yh], yrecv, CY_ID, yfar)
    total = cpart[core, x, yh] + xr1[yh] + xl1[yh]
    arrived(yrecv, CY_ID)
    total = total + yrecv[...]
    for a in range(2):
        for b in range(2):
            coarse_ref[a, b] = total[a * 64 : a * 64 + 64, b * 64 : b * 64 + 64]

    @pl.when(jnp.logical_not(own_across))
    def _():
        sent(unit, T_ID)

    sent(alist, A_ID)
    u = panel.at[0, 0]
    zu = pror.at[0, 0]
    sent(u, Y_ID)
    for k in (X_ID, X_ID + 4):
        sent(u, k)
        sent(u, k + 1)
        sent(u.at[lo_half], k + 2)
        sent(u.at[hi_half], k + 3)
    for n in range(8):
        sent(u, CORE_ID + n)
        sent(zu, PY_ID + n)
    for n in range(3):
        sent(zu, Z_ID + n)
        sent(zu, Z_ID + 4 + n)
    sent(zu.at[lo_half], Z_ID + 3)
    sent(zu.at[hi_half], Z_ID + 7)
    piece = q.at[0, pl.ds(0, 256)]
    sent(piece, rs_id(0, 0, 0))
    sent(piece, rs_id(0, 1, 1))
    for step in (1, 2, 3):
        for half in (0, 1):
            for way in (0, 1):
                sent(piece, rs_id(step, half, way))
    sent(crecv, CC_ID)
    sent(xr0, CX_ID)
    sent(xl0, CX_ID + 1)
    sent(xr1, CX_ID + 2)
    sent(xl1, CX_ID + 3)
    sent(yrecv, CY_ID)


def shards(op_tiles, op_rows, op_cols, op_count, pro_tiles, pro_cols, pro_live):
    vmem = pl.BlockSpec(memory_space=pltpu.VMEM)
    smem = pl.BlockSpec(memory_space=pltpu.SMEM)
    return pl.pallas_call(
        kernel,
        out_shape=(
            jax.ShapeDtypeStruct((8, 2, 64, 64), F32),
            jax.ShapeDtypeStruct((2, 2, 64, 64), F32),
        ),
        in_specs=[vmem, smem, smem, smem, vmem, smem, smem],
        out_specs=(vmem, vmem),
        scratch_shapes=[
            pltpu.VMEM((UR, 128), F32),
            pltpu.VMEM((LA + 1, 32, 128), F32),
            pltpu.VMEM((LA + 1, 32, 128), F32),
            pltpu.VMEM((2, 8, UR, 128), F32),
            pltpu.VMEM((2, 8, UR, 128), F32),
            pltpu.VMEM((2, 512, 512), BF16),
            pltpu.VMEM((2, 512, 512), BF16),
            pltpu.VMEM((2, 512, 256), BF16),
            pltpu.VMEM((2, 512, 256), BF16),
            pltpu.VMEM((8, 512, 128), F32),
            pltpu.VMEM((4, 512, 128), F32),
            pltpu.VMEM((4, 512, 128), F32),
            pltpu.VMEM((16, 128, 512), BF16),
            pltpu.VMEM((16, 128, 512), BF16),
            pltpu.VMEM((512, 128), BF16),
            pltpu.VMEM((512, 128), BF16),
            pltpu.VMEM((2, 4, 2, 128, 128), F32),
            pltpu.VMEM((4, 2, 128, 128), F32),
            pltpu.VMEM((128, 128), F32),
            pltpu.VMEM((128, 128), F32),
            pltpu.VMEM((2, 128, 128), F32),
            pltpu.VMEM((2, 128, 128), F32),
            pltpu.VMEM((128, 128), F32),
            pltpu.SemaphoreType.DMA((N_ID,)),
            pltpu.SemaphoreType.DMA((N_ID,)),
            pltpu.SemaphoreType.DMA((2,)),
        ],
        compiler_params=pltpu.CompilerParams(
            collective_id=0, has_side_effects=True, vmem_limit_bytes=60 * 1024 * 1024
        ),
    )(
        op_tiles.reshape(32, 64, 64), op_rows, op_cols, op_count,
        pro_tiles.reshape(8, 64, 64), pro_cols, pro_live,
    )


def solution(mesh):
    return jax.shard_map(
        shards,
        mesh=mesh,
        in_specs=(
            P("row", "col", None, None),
            P("row", "col"),
            P("row", "col"),
            P("row", "col"),
            P("row", "col", None, None),
            P("row", "col"),
            P("row", "col"),
        ),
        out_specs=(P("row", "col", None, None), P("row", "col", None, None)),
        check_vma=False,
    )
```

```python
import functools

import jax
import jax.numpy as jnp
from jax import lax
from jax.experimental import pallas as pl
from jax.experimental.pallas import tpu as pltpu
from jax.sharding import PartitionSpec as P

MESH = pl.DeviceIdType.MESH
F32, BF16 = jnp.float32, jnp.bfloat16
UR = 264
UH = 136
LA = 32
HALF = ((0, 256), (256, 256))

M_ID, T_ID, Y_ID = 0, 1, 2
X_ID = 3
CORE_ID = 11
Z_ID = 19
PY_ID = 27
RS_ID = 35
CC_ID = 51
CX_ID = 55
CY_ID = 59
A_ID = 60
N_ID = 64


def split(v):
    hi = v.astype(BF16)
    return hi, (v - hi.astype(F32)).astype(BF16)


def pack(tile):
    return jnp.concatenate([tile[:32], tile[32:]], axis=1)


def kernel(
    op_hbm, rows_ref, cols_ref, count_ref, pro_ref, pcols_ref, plive_ref,
    prod_hbm, coarse_ref,
    op_ref, prod_ref, meta, mnear,
    unit, alist, anear, panel, pror, ahi, alo, rhi, rlo, q, rsr, rsl, pthi, ptlo, pcat,
    cpart, crecv, xr0, xl0, xr1, xl1, yrecv,
    ssem, rsem, lsem,
):
    r = lax.axis_index("row")
    c = lax.axis_index("col")
    yh, x, core = r // 8, lax.rem(r // 2, 4), lax.rem(r, 2)
    yl, z = c // 8, lax.rem(c, 8)

    def rowdev(yh_, x_, core_):
        return ((yh_ * 4 + x_) * 2 + core_, c)

    ynear = (r, (1 - yl) * 8 + z)
    zright, zleft = (r, yl * 8 + lax.rem(z + 1, 8)), (r, yl * 8 + lax.rem(z + 7, 8))
    xright, xleft = rowdev(yh, lax.rem(x + 1, 4), core), rowdev(yh, lax.rem(x + 3, 4), core)
    yfar = rowdev(1 - yh, x, core)
    other = rowdev(yh, x, 1 - core)
    s0 = 2 * x + core
    across = ((yh * 4 + z // 2) * 2 + lax.rem(z, 2), yl * 8 + s0)
    own_across = s0 == z

    def send(src, dst, k, dev):
        pltpu.make_async_remote_copy(
            src_ref=src, dst_ref=dst, send_sem=ssem.at[k], recv_sem=rsem.at[k], device_id=dev, device_id_type=MESH
        ).start()

    def arrived(dst, k):
        pltpu.make_async_remote_copy(
            src_ref=dst, dst_ref=dst, send_sem=ssem.at[k], recv_sem=rsem.at[k], device_id=ynear, device_id_type=MESH
        ).wait_recv()

    def sent(src, k):
        pltpu.make_async_remote_copy(
            src_ref=src, dst_ref=src, send_sem=ssem.at[k], recv_sem=rsem.at[k], device_id=ynear, device_id_type=MESH
        ).wait_send()

    fetch = pltpu.make_async_copy(op_hbm, op_ref, lsem.at[2])
    fetch.start()
    barrier = pltpu.get_barrier_semaphore()
    for dev in (ynear, zright, zleft, xright, xleft, yfar, other):
        pl.semaphore_signal(barrier, inc=1, device_id=dev, device_id_type=MESH)

    @pl.when(jnp.logical_not(own_across))
    def _():
        pl.semaphore_signal(barrier, inc=1, device_id=across, device_id_type=MESH)

    for k in range(8):
        live = plive_ref[0, k].astype(F32)
        unit[pl.ds(k * 32, 32), :] = pack(pro_ref[k]) * live
        unit[pl.ds(256 + k, 1), :] = jnp.full((1, 128), pcols_ref[0, k].astype(F32))

    pl.semaphore_wait(barrier, jnp.where(own_across, 7, 8))

    @pl.when(own_across)
    def _():
        pltpu.make_async_copy(unit, panel.at[yh, z], lsem.at[0]).start()

    @pl.when(jnp.logical_not(own_across))
    def _():
        send(unit, panel.at[yh, z], T_ID, across)

    keep = pltpu.make_async_copy(unit, pror.at[yl, z], lsem.at[1])
    keep.start()

    pos = rows_ref[...] * 8 + cols_ref[...]
    live_slot = lax.broadcasted_iota(jnp.int32, (1, LA), 1) < count_ref[0, 0]
    pos = jnp.where(live_slot, pos, -1).astype(F32)
    meta[...] = jnp.zeros((8, 128), F32)
    meta[pl.ds(0, 1), pl.ds(0, LA)] = pos
    meta[pl.ds(0, 1), pl.ds(LA, LA)] = pos
    send(meta, mnear, M_ID, ynear)
    fetch.wait()

    def pack_piece(n):
        def slot(t, carry):
            a = op_ref[t, pl.ds(n * 8, 8), :]
            b = op_ref[t, pl.ds(32 + n * 8, 8), :]
            alist[pl.ds(n * 8, 8), t, :] = jnp.concatenate([a, b], axis=1)
            return carry

        lax.fori_loop(0, LA, slot, 0, unroll=8)

    def send_piece(n):
        at = pl.ds(n * 8, 8)
        send(alist.at[at], anear.at[at], A_ID + n, ynear)

    for n in range(4):
        pack_piece(n)
        if n < 2:
            send_piece(n)

    left32 = lax.broadcasted_iota(jnp.int32, (32, 128), 1) < 64
    left8 = lax.broadcasted_iota(jnp.int32, (8, 128), 1) < 64
    place = lax.broadcasted_iota(jnp.int32, (64, 2 * LA), 0)
    place = (lax.rem(place, 8) * 8 + place // 8).astype(F32)

    def dot(a, b):
        return lax.dot_general(a, b, (((1,), (0,)), ((), ())), preferred_element_type=F32)

    def build_a(src, which, at, n):
        hot = (which[pl.ds(0, 1), pl.ds(0, 2 * LA)] == place).astype(F32).astype(BF16)

        def row(step, carry):
            rho = n * 8 + step * 2
            h0, l0 = split(src[rho])
            h1, l1 = split(src[rho + 1])
            both = jnp.concatenate(
                [jnp.concatenate([h0, l0], axis=0), jnp.concatenate([h1, l1], axis=0)], axis=1
            )
            tiles = dot(hot, both)
            for e in range(2):
                t = tiles[:, e * 128 : e * 128 + 128]
                for m in range(4):
                    even, odd = t[m * 16 : m * 16 + 8], t[m * 16 + 8 : m * 16 + 16]
                    top = jnp.where(left8, even, pltpu.roll(odd, 64, 1))
                    bot = jnp.where(left8, pltpu.roll(even, 64, 1), odd)
                    hi, lo = split(jnp.concatenate([top, bot], axis=0))
                    at_rows = pl.ds(pl.multiple_of((rho + e) * 16, 16), 16)
                    ahi[at, at_rows, pl.ds(m * 128, 128)] = hi
                    alo[at, at_rows, pl.ds(m * 128, 128)] = lo
            return carry

        lax.fori_loop(0, 4, row, 0)

    def dense(ref, b, s, k):
        tile = ref[b, s, pl.ds(k * 32, 32), :]
        col = ref[b, s, pl.ds(256 + k, 1), :]
        turned = pltpu.roll(tile, 64, 1)
        a, bb = 1.0 - col, col
        top = jnp.where(left32, tile * a, turned * bb)
        bot = jnp.where(left32, turned * a, tile * bb)
        return top, bot

    build_a(alist, meta, yl, 0)

    @pl.when(own_across)
    def _():
        pltpu.make_async_copy(unit, panel.at[yh, z], lsem.at[0]).wait()

    @pl.when(jnp.logical_not(own_across))
    def _():
        arrived(panel.at[yh, s0], T_ID)

    sl, sr = lax.rem(s0 + 6, 8), lax.rem(s0 + 2, 8)
    sf = lax.rem(s0 + 4, 8)
    lo_half, hi_half = pl.ds(0, UH), pl.ds(UH, UR - UH)

    def spread(b, k):
        u = panel.at[b, s0]
        send(u, u, k, xright)
        send(u, u, k + 1, xleft)

    mine, theirs = yh, 1 - yh
    u = panel.at[mine, s0]
    send(u, u, Y_ID, yfar)
    send_piece(2)
    send_piece(3)
    spread(mine, X_ID)
    send(u, u, CORE_ID, other)
    keep.wait()
    zu = pror.at[yl, z]
    send(zu, zu, Z_ID, zright)
    send(zu, zu, Z_ID + 4, zleft)

    def pass_on(b, k, kc):
        u = panel.at[b, sl]
        arrived(u, k)
        send(u.at[lo_half], u.at[lo_half], k + 2, xright)
        send(u, u, kc, other)
        u = panel.at[b, sr]
        arrived(u, k + 1)
        send(u.at[hi_half], u.at[hi_half], k + 3, xleft)
        send(u, u, kc + 1, other)

    def zstep(step):
        got_r = pror.at[yl, lax.rem(z + 8 - step, 8)]
        got_l = pror.at[yl, lax.rem(z + step, 8)]
        arrived(got_r, Z_ID + step - 1)
        arrived(got_l, Z_ID + 4 + step - 1)
        if step < 3:
            send(got_r, got_r, Z_ID + step, zright)
            send(got_l, got_l, Z_ID + 4 + step, zleft)
        else:
            send(got_r.at[lo_half], got_r.at[lo_half], Z_ID + 3, zright)
            send(got_l.at[hi_half], got_l.at[hi_half], Z_ID + 7, zleft)

    for n in range(1, 4):
        build_a(alist, meta, yl, n)
    pass_on(mine, X_ID, CORE_ID + 1)
    u = panel.at[theirs, s0]
    arrived(u, Y_ID)
    spread(theirs, X_ID + 4)
    send(u, u, CORE_ID + 4, other)
    zstep(1)
    arrived(mnear, M_ID)
    for n in range(2):
        arrived(anear.at[pl.ds(n * 8, 8)], A_ID + n)
        build_a(anear, mnear, 1 - yl, n)
    far = panel.at[mine, sf]
    arrived(far.at[lo_half], X_ID + 2)
    arrived(far.at[hi_half], X_ID + 3)
    send(far, far, CORE_ID + 3, other)
    pass_on(theirs, X_ID + 4, CORE_ID + 5)
    zstep(2)
    far2 = panel.at[theirs, sf]
    arrived(far2.at[lo_half], X_ID + 6)
    arrived(far2.at[hi_half], X_ID + 7)
    send(far2, far2, CORE_ID + 7, other)
    zstep(3)
    for n in range(2, 4):
        arrived(anear.at[pl.ds(n * 8, 8)], A_ID + n)
        build_a(anear, mnear, 1 - yl, n)
    send(zu, zu, PY_ID, ynear)
    for step in (1, 2, 3):
        got_r = pror.at[yl, lax.rem(z + 8 - step, 8)]
        got_l = pror.at[yl, lax.rem(z + step, 8)]
        send(got_r, got_r, PY_ID + 2 * step - 1, ynear)
        send(got_l, got_l, PY_ID + 2 * step, ynear)
    o0 = 2 * x + 1 - core
    from_other = [
        panel.at[b, lax.rem(o0 + off, 8)] for b in (mine, theirs) for off in (0, 6, 2, 4)
    ]
    for n, ref in enumerate(from_other):
        arrived(ref, CORE_ID + n)

    def build_r(d, at):
        s = lax.rem(z + d, 8)

        def block(b, carry):
            for k in range(8):
                for off, v in zip((0, 32), dense(panel, b, s, k)):
                    hi, lo = split(v)
                    rhi[b, pl.ds(k * 64 + off, 32), pl.ds(at * 128, 128)] = hi
                    rlo[b, pl.ds(k * 64 + off, 32), pl.ds(at * 128, 128)] = lo
            return carry

        lax.fori_loop(0, 2, block, 0)

    def chunk(d0, d1):
        build_r(d0, 0)
        build_r(d1, 1)

        def part(m, carry):
            rows = pl.ds(pl.multiple_of(m * 256, 256), 256)
            acc = jnp.zeros((256, 256), F32)
            for b in range(2):
                h, l = ahi[b, rows, :], alo[b, rows, :]
                acc = acc + dot(h, rhi[b]) + dot(h, rlo[b]) + dot(l, rhi[b])
            q[d0, rows, :] = acc[:, :128]
            q[d1, rows, :] = acc[:, 128:]
            return carry

        lax.fori_loop(0, 2, part, 0)

    def rs_id(step, half, way):
        return RS_ID + (step * 2 + half) * 2 + way

    def rs_send(d, step, half, way):
        rows = pl.ds(*HALF[half])
        buf = (rsr, rsl)[way]
        send(q.at[d, rows], buf.at[step, rows], rs_id(step, half, way), (zright, zleft)[way])

    def rs_add(d, step, half, way):
        rows = pl.ds(*HALF[half])
        buf = (rsr, rsl)[way]
        arrived(buf.at[step, rows], rs_id(step, half, way))
        q[d, rows, :] = q[d, rows, :] + buf[step, rows, :]

    def build_t(b, s):
        flag = pror[b, s, pl.ds(256, 8), :]
        for m in range(4):
            parts = []
            for rho in range(8 * m, 8 * m + 8):
                tile = pror[b, s, pl.ds(rho, 8, stride=32), :]
                turned = pltpu.roll(tile, 64, 1)
                parts.append(jnp.where(left8, tile * (1.0 - flag), turned * flag))
                parts.append(jnp.where(left8, turned * (1.0 - flag), tile * flag))
            hi, lo = split(jnp.concatenate(parts, axis=0).T)
            g = b * 8 + s
            rows = pl.ds(pl.multiple_of(g // 8 * 128, 128), 128)
            pthi[lax.rem(g, 2), lax.rem(g // 2, 4), rows, pl.ds(m * 128, 128)] = hi
            ptlo[lax.rem(g, 2), lax.rem(g // 2, 4), rows, pl.ds(m * 128, 128)] = lo

    chunk(4, 0)
    rs_send(4, 0, 0, 0)
    rs_send(4, 0, 1, 1)
    chunk(3, 5)
    rs_send(3, 1, 1, 0)
    rs_send(5, 1, 0, 1)
    rs_add(3, 0, 0, 0)
    rs_send(3, 1, 0, 0)
    rs_add(5, 0, 1, 1)
    rs_send(5, 1, 1, 1)
    chunk(2, 6)

    zfar = pror.at[yl, lax.rem(z + 4, 8)]
    arrived(zfar.at[lo_half], Z_ID + 3)
    arrived(zfar.at[hi_half], Z_ID + 7)
    send(zfar, zfar, PY_ID + 7, ynear)

    for half_r, half_l in ((1, 0), (0, 1)):
        rs_add(2, 1, half_r, 0)
        rs_send(2, 2, half_r, 0)
        rs_add(6, 1, half_l, 1)
        rs_send(6, 2, half_l, 1)
    chunk(1, 7)

    def own_t(s, carry):
        build_t(yl, s)
        return carry

    for half_r, half_l in ((1, 0), (0, 1)):
        rs_add(1, 2, half_r, 0)
        rs_send(1, 3, half_r, 0)
        rs_add(7, 2, half_l, 1)
        rs_send(7, 3, half_l, 1)
    lax.fori_loop(0, 8, own_t, 0)

    near = [pror.at[1 - yl, z]]
    for step in (1, 2, 3):
        near += [pror.at[1 - yl, lax.rem(z + 8 - step, 8)], pror.at[1 - yl, lax.rem(z + step, 8)]]
    near.append(pror.at[1 - yl, lax.rem(z + 4, 8)])
    for n, ref in enumerate(near):
        arrived(ref, PY_ID + n)

    def near_t(s, carry):
        build_t(1 - yl, s)
        return carry

    lax.fori_loop(0, 8, near_t, 0)

    for half in (0, 1):
        rs_add(0, 3, half, 0)
        rs_add(0, 3, half, 1)
        rows = pl.ds(*HALF[half])
        hi, lo = split(q[0, rows, :])
        pcat[rows, pl.ds(0, 128)] = hi
        pcat[rows, pl.ds(128, 128)] = lo

    def coarse_part(gc, gx):
        v = dot(pthi[gc, gx], pcat[...])
        v = v[:, :128] + v[:, 128:] + dot(ptlo[gc, gx], pcat[:, :128])
        cpart[gc, gx, 0] = v[:128]
        cpart[gc, gx, 1] = v[128:]

    def to_other(gx, n):
        coarse_part(1 - core, gx)
        send(cpart.at[1 - core, gx], crecv.at[gx], CC_ID + n, other)

    def from_core(gx, n):
        coarse_part(core, gx)
        arrived(crecv.at[gx], CC_ID + n)
        cpart[core, gx] = cpart[core, gx] + crecv[gx]

    x2 = lax.rem(x + 2, 4)
    xp, xm = lax.rem(x + 1, 4), lax.rem(x + 3, 4)
    cp = cpart.at[core]
    to_other(x2, 0)
    to_other(xp, 1)
    from_core(x2, 0)
    send(cp.at[x2, 0], xr0, CX_ID, xright)
    send(cp.at[x2, 1], xl0, CX_ID + 1, xleft)
    to_other(xm, 2)
    from_core(xp, 1)
    to_other(x, 3)
    from_core(xm, 2)
    arrived(xr0, CX_ID)
    cpart[core, xp, 0] = cpart[core, xp, 0] + xr0[...]
    send(cp.at[xp], xr1, CX_ID + 2, xright)
    arrived(xl0, CX_ID + 1)
    cpart[core, xm, 1] = cpart[core, xm, 1] + xl0[...]
    send(cp.at[xm], xl1, CX_ID + 3, xleft)
    from_core(x, 3)
    for i in range(8):
        for h in range(2):
            v = q[0, pl.ds(h * 8 + i, 32, stride=16), :]
            prod_ref[i, 0, pl.ds(h * 32, 32), :] = v[:, :64]
            prod_ref[i, 1, pl.ds(h * 32, 32), :] = v[:, 64:]
    put = pltpu.make_async_copy(prod_ref, prod_hbm, lsem.at[3])
    put.start()
    arrived(xr1, CX_ID + 2)
    arrived(xl1, CX_ID + 3)
    cpart[core, x, 1 - yh] = cpart[core, x, 1 - yh] + xr1[1 - yh] + xl1[1 - yh]
    send(cp.at[x, 1 - yh], yrecv, CY_ID, yfar)
    total = cpart[core, x, yh] + xr1[yh] + xl1[yh]
    arrived(yrecv, CY_ID)
    total = total + yrecv[...]
    for a in range(2):
        for b in range(2):
            coarse_ref[a, b] = total[a * 64 : a * 64 + 64, b * 64 : b * 64 + 64]

    @pl.when(jnp.logical_not(own_across))
    def _():
        sent(unit, T_ID)

    put.wait()
    sent(meta, M_ID)
    for n in range(4):
        sent(alist.at[pl.ds(0, 8)], A_ID + n)
    u = panel.at[0, 0]
    zu = pror.at[0, 0]
    sent(u, Y_ID)
    for k in (X_ID, X_ID + 4):
        sent(u, k)
        sent(u, k + 1)
        sent(u.at[lo_half], k + 2)
        sent(u.at[hi_half], k + 3)
    for n in range(8):
        sent(u, CORE_ID + n)
        sent(zu, PY_ID + n)
    for n in range(3):
        sent(zu, Z_ID + n)
        sent(zu, Z_ID + 4 + n)
    sent(zu.at[lo_half], Z_ID + 3)
    sent(zu.at[hi_half], Z_ID + 7)
    piece = q.at[0, pl.ds(0, 256)]
    sent(piece, rs_id(0, 0, 0))
    sent(piece, rs_id(0, 1, 1))
    for step in (1, 2, 3):
        for half in (0, 1):
            for way in (0, 1):
                sent(piece, rs_id(step, half, way))
    for n in range(4):
        sent(crecv.at[0], CC_ID + n)
    sent(xr0, CX_ID)
    sent(xl0, CX_ID + 1)
    sent(xr1, CX_ID + 2)
    sent(xl1, CX_ID + 3)
    sent(yrecv, CY_ID)


def shards(op_tiles, op_rows, op_cols, op_count, pro_tiles, pro_cols, pro_live):
    vmem = pl.BlockSpec(memory_space=pltpu.VMEM)
    smem = pl.BlockSpec(memory_space=pltpu.SMEM)
    anywhere = pl.BlockSpec(memory_space=pl.ANY)
    return pl.pallas_call(
        kernel,
        out_shape=(
            jax.ShapeDtypeStruct((8, 2, 64, 64), F32),
            jax.ShapeDtypeStruct((2, 2, 64, 64), F32),
        ),
        in_specs=[anywhere, vmem, vmem, smem, vmem, smem, smem],
        out_specs=(anywhere, vmem),
        scratch_shapes=[
            pltpu.VMEM((LA, 64, 64), F32),
            pltpu.VMEM((8, 2, 64, 64), F32),
            pltpu.VMEM((8, 128), F32),
            pltpu.VMEM((8, 128), F32),
            pltpu.VMEM((UR, 128), F32),
            pltpu.VMEM((32, LA, 128), F32),
            pltpu.VMEM((32, LA, 128), F32),
            pltpu.VMEM((2, 8, UR, 128), F32),
            pltpu.VMEM((2, 8, UR, 128), F32),
            pltpu.VMEM((2, 512, 512), BF16),
            pltpu.VMEM((2, 512, 512), BF16),
            pltpu.VMEM((2, 512, 256), BF16),
            pltpu.VMEM((2, 512, 256), BF16),
            pltpu.VMEM((8, 512, 128), F32),
            pltpu.VMEM((4, 512, 128), F32),
            pltpu.VMEM((4, 512, 128), F32),
            pltpu.VMEM((2, 4, 256, 512), BF16),
            pltpu.VMEM((2, 4, 256, 512), BF16),
            pltpu.VMEM((512, 256), BF16),
            pltpu.VMEM((2, 4, 2, 128, 128), F32),
            pltpu.VMEM((4, 2, 128, 128), F32),
            pltpu.VMEM((128, 128), F32),
            pltpu.VMEM((128, 128), F32),
            pltpu.VMEM((2, 128, 128), F32),
            pltpu.VMEM((2, 128, 128), F32),
            pltpu.VMEM((128, 128), F32),
            pltpu.SemaphoreType.DMA((N_ID,)),
            pltpu.SemaphoreType.DMA((N_ID,)),
            pltpu.SemaphoreType.DMA((4,)),
        ],
        compiler_params=pltpu.CompilerParams(
            collective_id=0, has_side_effects=True, vmem_limit_bytes=60 * 1024 * 1024
        ),
    )(
        op_tiles.reshape(32, 64, 64), op_rows.T, op_cols.T, op_count,
        pro_tiles.reshape(8, 64, 64), pro_cols.T, pro_live.T,
    )


def solution(mesh):
    return jax.shard_map(
        shards,
        mesh=mesh,
        in_specs=(
            P("row", "col", None, None),
            P("row", "col"),
            P("row", "col"),
            P("row", "col"),
            P("row", "col", None, None),
            P("row", "col"),
            P("row", "col"),
        ),
        out_specs=(P("row", "col", None, None), P("row", "col", None, None)),
        check_vma=False,
    )
```

```python
import functools

import jax
import jax.numpy as jnp
from jax import lax
from jax.experimental import pallas as pl
from jax.experimental.pallas import tpu as pltpu
from jax.sharding import PartitionSpec as P

MESH = pl.DeviceIdType.MESH
F32, BF16 = jnp.float32, jnp.bfloat16
UR = 264
UH = 136
LA = 32
HALF = ((0, 256), (256, 256))
PART = (pl.ds(0, UH), pl.ds(UH, UR - UH))

M_ID = 0
A_ID = 1
T_ID = 5
Y_ID = 7
X_ID = 9
CORE_ID = 21
Z_ID = 29
PY_ID = 37
RS_ID = 45
CC_ID = 61
CX_ID = 65
CY_ID = 73
N_ID = 75


def split(v):
    hi = v.astype(BF16)
    return hi, (v - hi.astype(F32)).astype(BF16)


def pack(tile):
    return jnp.concatenate([tile[:32], tile[32:]], axis=1)


def kernel(
    op_hbm, rows_ref, cols_ref, count_ref, pro_ref, pcols_ref, plive_ref,
    prod_hbm, coarse_ref,
    op_ref, prod_ref, meta, mnear,
    unit, alist, anear, panel, pror, ahi, alo, rhi, rlo, q, rsr, rsl, pthi, ptlo, pcat,
    cpart, crecv, xr0, xl0, xr1, xl1, yrecv,
    ssem, rsem, lsem,
):
    r = lax.axis_index("row")
    c = lax.axis_index("col")
    yh, x, core = r // 8, lax.rem(r // 2, 4), lax.rem(r, 2)
    yl, z = c // 8, lax.rem(c, 8)

    def rowdev(yh_, x_, core_):
        return ((yh_ * 4 + x_) * 2 + core_, c)

    ynear = (r, (1 - yl) * 8 + z)
    zright, zleft = (r, yl * 8 + lax.rem(z + 1, 8)), (r, yl * 8 + lax.rem(z + 7, 8))
    xright, xleft = rowdev(yh, lax.rem(x + 1, 4), core), rowdev(yh, lax.rem(x + 3, 4), core)
    yfar = rowdev(1 - yh, x, core)
    other = rowdev(yh, x, 1 - core)
    s0 = 4 * core + x
    plane = 2 * x + core
    across = rowdev(yh, lax.rem(z, 4), z // 4)[0], yl * 8 + plane
    source = rowdev(yh, z // 2, lax.rem(z, 2))[0], yl * 8 + s0
    own_across = jnp.logical_and(s0 == z, plane == z)

    def send(src, dst, k, dev):
        pltpu.make_async_remote_copy(
            src_ref=src, dst_ref=dst, send_sem=ssem.at[k], recv_sem=rsem.at[k], device_id=dev, device_id_type=MESH
        ).start()

    def arrived(dst, k):
        pltpu.make_async_remote_copy(
            src_ref=dst, dst_ref=dst, send_sem=ssem.at[k], recv_sem=rsem.at[k], device_id=ynear, device_id_type=MESH
        ).wait_recv()

    def sent(src, k):
        pltpu.make_async_remote_copy(
            src_ref=src, dst_ref=src, send_sem=ssem.at[k], recv_sem=rsem.at[k], device_id=ynear, device_id_type=MESH
        ).wait_send()

    fetch = pltpu.make_async_copy(op_hbm, op_ref, lsem.at[2])
    fetch.start()
    barrier = pltpu.get_barrier_semaphore()
    for dev in (ynear, zright, zleft, xright, xleft, yfar, other):
        pl.semaphore_signal(barrier, inc=1, device_id=dev, device_id_type=MESH)

    @pl.when(jnp.logical_not(own_across))
    def _():
        pl.semaphore_signal(barrier, inc=1, device_id=across, device_id_type=MESH)
        pl.semaphore_signal(barrier, inc=1, device_id=source, device_id_type=MESH)

    for k in range(8):
        live = plive_ref[0, k].astype(F32)
        unit[pl.ds(k * 32, 32), :] = pack(pro_ref[k]) * live
        unit[pl.ds(256 + k, 1), :] = jnp.full((1, 128), pcols_ref[0, k].astype(F32))

    pl.semaphore_wait(barrier, jnp.where(own_across, 7, 9))

    @pl.when(own_across)
    def _():
        pltpu.make_async_copy(unit, panel.at[yh, z], lsem.at[0]).start()

    @pl.when(jnp.logical_not(own_across))
    def _():
        for p in range(2):
            send(unit.at[PART[p]], panel.at[yh, z].at[PART[p]], T_ID + p, across)

    keep = pltpu.make_async_copy(unit, pror.at[yl, z], lsem.at[1])
    keep.start()

    pos = rows_ref[...] * 8 + cols_ref[...]
    live_slot = lax.broadcasted_iota(jnp.int32, (1, LA), 1) < count_ref[0, 0]
    pos = jnp.where(live_slot, pos, -1).astype(F32)
    meta[...] = jnp.zeros((8, 128), F32)
    meta[pl.ds(0, 1), pl.ds(0, LA)] = pos
    meta[pl.ds(0, 1), pl.ds(LA, LA)] = pos
    send(meta, mnear, M_ID, ynear)
    fetch.wait()

    def pack_piece(n):
        def slot(t, carry):
            a = op_ref[t, pl.ds(n * 8, 8), :]
            b = op_ref[t, pl.ds(32 + n * 8, 8), :]
            alist[pl.ds(n * 8, 8), t, :] = jnp.concatenate([a, b], axis=1)
            return carry

        lax.fori_loop(0, LA, slot, 0, unroll=8)

    def send_piece(n):
        at = pl.ds(n * 8, 8)
        send(alist.at[at], anear.at[at], A_ID + n, ynear)

    for n in range(4):
        pack_piece(n)
        if n < 2:
            send_piece(n)

    left32 = lax.broadcasted_iota(jnp.int32, (32, 128), 1) < 64
    left8 = lax.broadcasted_iota(jnp.int32, (8, 128), 1) < 64
    place = lax.broadcasted_iota(jnp.int32, (64, 2 * LA), 0)
    place = (lax.rem(place, 8) * 8 + place // 8).astype(F32)

    def dot(a, b):
        return lax.dot_general(a, b, (((1,), (0,)), ((), ())), preferred_element_type=F32)

    def build_a(src, which, at, n):
        hot = (which[pl.ds(0, 1), pl.ds(0, 2 * LA)] == place).astype(F32).astype(BF16)

        def row(step, carry):
            rho = n * 8 + step * 2
            h0, l0 = split(src[rho])
            h1, l1 = split(src[rho + 1])
            both = jnp.concatenate(
                [jnp.concatenate([h0, l0], axis=0), jnp.concatenate([h1, l1], axis=0)], axis=1
            )
            tiles = dot(hot, both)
            for e in range(2):
                t = tiles[:, e * 128 : e * 128 + 128]
                for m in range(4):
                    even, odd = t[m * 16 : m * 16 + 8], t[m * 16 + 8 : m * 16 + 16]
                    top = jnp.where(left8, even, pltpu.roll(odd, 64, 1))
                    bot = jnp.where(left8, pltpu.roll(even, 64, 1), odd)
                    hi, lo = split(jnp.concatenate([top, bot], axis=0))
                    at_rows = pl.ds(pl.multiple_of((rho + e) * 16, 16), 16)
                    ahi[at, at_rows, pl.ds(m * 128, 128)] = hi
                    alo[at, at_rows, pl.ds(m * 128, 128)] = lo
            return carry

        lax.fori_loop(0, 4, row, 0)

    def dense(ref, b, s, k):
        tile = ref[b, s, pl.ds(k * 32, 32), :]
        col = ref[b, s, pl.ds(256 + k, 1), :]
        turned = pltpu.roll(tile, 64, 1)
        a, bb = 1.0 - col, col
        top = jnp.where(left32, tile * a, turned * bb)
        bot = jnp.where(left32, turned * a, tile * bb)
        return top, bot

    build_a(alist, meta, yl, 0)

    def ring(off):
        return 4 * core + lax.rem(x + off, 4)

    mine, theirs = yh, 1 - yh
    sl, sr, sf = ring(3), ring(1), ring(2)

    def spread(b, k, p):
        u = panel.at[b, s0].at[PART[p]]
        send(u, u, k + p, xright)
        send(u, u, k + 2 + p, xleft)

    def onward(b, k):
        u = panel.at[b, sl].at[PART[0]]
        arrived(u, k)
        send(u, u, k + 4, xright)
        u = panel.at[b, sr].at[PART[1]]
        arrived(u, k + 3)
        send(u, u, k + 5, xleft)

    def beside(b, k, kc):
        u = panel.at[b, sl]
        arrived(u.at[PART[1]], k + 1)
        send(u, u, kc + 1, other)
        u = panel.at[b, sr]
        arrived(u.at[PART[0]], k + 2)
        send(u, u, kc + 2, other)

    def far(b, k, kc):
        u = panel.at[b, sf]
        arrived(u.at[PART[0]], k + 4)
        arrived(u.at[PART[1]], k + 5)
        send(u, u, kc + 3, other)

    def zstep(step):
        got_r = pror.at[yl, lax.rem(z + 8 - step, 8)]
        got_l = pror.at[yl, lax.rem(z + step, 8)]
        arrived(got_r, Z_ID + step - 1)
        arrived(got_l, Z_ID + 4 + step - 1)
        if step < 3:
            send(got_r, got_r, Z_ID + step, zright)
            send(got_l, got_l, Z_ID + 4 + step, zleft)
        else:
            send(got_r.at[PART[0]], got_r.at[PART[0]], Z_ID + 3, zright)
            send(got_l.at[PART[1]], got_l.at[PART[1]], Z_ID + 7, zleft)
        send(got_r, got_r, PY_ID + 2 * step - 1, ynear)
        send(got_l, got_l, PY_ID + 2 * step, ynear)

    u = panel.at[mine, s0]

    @pl.when(own_across)
    def _():
        pltpu.make_async_copy(unit, panel.at[yh, z], lsem.at[0]).wait()

    for p in range(2):
        @pl.when(jnp.logical_not(own_across))
        def _():
            arrived(u.at[PART[p]], T_ID + p)

        send(u.at[PART[p]], u.at[PART[p]], Y_ID + p, yfar)
        spread(mine, X_ID, p)
    send_piece(2)
    send_piece(3)
    send(u, u, CORE_ID, other)
    keep.wait()
    zu = pror.at[yl, z]
    send(zu, zu, Z_ID, zright)
    send(zu, zu, Z_ID + 4, zleft)
    send(zu, zu, PY_ID, ynear)
    build_a(alist, meta, yl, 1)
    onward(mine, X_ID)
    build_a(alist, meta, yl, 2)
    u = panel.at[theirs, s0]
    for p in range(2):
        arrived(u.at[PART[p]], Y_ID + p)
        spread(theirs, X_ID + 6, p)
    send(u, u, CORE_ID + 4, other)
    beside(mine, X_ID, CORE_ID)
    zstep(1)
    build_a(alist, meta, yl, 3)
    onward(theirs, X_ID + 6)
    far(mine, X_ID, CORE_ID)
    arrived(mnear, M_ID)
    for n in range(2):
        arrived(anear.at[pl.ds(n * 8, 8)], A_ID + n)
        build_a(anear, mnear, 1 - yl, n)
    beside(theirs, X_ID + 6, CORE_ID + 4)
    zstep(2)
    far(theirs, X_ID + 6, CORE_ID + 4)
    for n in range(2, 4):
        arrived(anear.at[pl.ds(n * 8, 8)], A_ID + n)
        build_a(anear, mnear, 1 - yl, n)
    for n in range(8):
        s = 4 * (1 - core) + lax.rem(x + (0, 3, 1, 2)[n % 4], 4)
        arrived(panel.at[(mine, theirs)[n // 4], s], CORE_ID + n)

    def build_r(d, at):
        s = lax.rem(z + d, 8)

        def block(b, carry):
            for k in range(8):
                for off, v in zip((0, 32), dense(panel, b, s, k)):
                    hi, lo = split(v)
                    rhi[b, pl.ds(k * 64 + off, 32), pl.ds(at * 128, 128)] = hi
                    rlo[b, pl.ds(k * 64 + off, 32), pl.ds(at * 128, 128)] = lo
            return carry

        lax.fori_loop(0, 2, block, 0)

    def chunk(d0, d1):
        build_r(d0, 0)
        build_r(d1, 1)

        def part(m, carry):
            rows = pl.ds(pl.multiple_of(m * 256, 256), 256)
            acc = jnp.zeros((256, 256), F32)
            for b in range(2):
                h, l = ahi[b, rows, :], alo[b, rows, :]
                acc = acc + dot(h, rhi[b]) + dot(h, rlo[b]) + dot(l, rhi[b])
            q[d0, rows, :] = acc[:, :128]
            q[d1, rows, :] = acc[:, 128:]
            return carry

        lax.fori_loop(0, 2, part, 0)

    def rs_id(step, half, way):
        return RS_ID + (step * 2 + half) * 2 + way

    def rs_send(d, step, half, way):
        rows = pl.ds(*HALF[half])
        buf = (rsr, rsl)[way]
        send(q.at[d, rows], buf.at[step, rows], rs_id(step, half, way), (zright, zleft)[way])

    def rs_add(d, step, half, way):
        rows = pl.ds(*HALF[half])
        buf = (rsr, rsl)[way]
        arrived(buf.at[step, rows], rs_id(step, half, way))
        q[d, rows, :] = q[d, rows, :] + buf[step, rows, :]

    def build_t(b, s):
        flag = pror[b, s, pl.ds(256, 8), :]
        for m in range(4):
            parts = []
            for rho in range(8 * m, 8 * m + 8):
                tile = pror[b, s, pl.ds(rho, 8, stride=32), :]
                turned = pltpu.roll(tile, 64, 1)
                parts.append(jnp.where(left8, tile * (1.0 - flag), turned * flag))
                parts.append(jnp.where(left8, turned * (1.0 - flag), tile * flag))
            hi, lo = split(jnp.concatenate(parts, axis=0).T)
            g = b * 8 + s
            rows = pl.ds(pl.multiple_of(g // 8 * 128, 128), 128)
            pthi[lax.rem(g, 2), lax.rem(g // 2, 4), rows, pl.ds(m * 128, 128)] = hi
            ptlo[lax.rem(g, 2), lax.rem(g // 2, 4), rows, pl.ds(m * 128, 128)] = lo

    chunk(4, 0)
    rs_send(4, 0, 0, 0)
    rs_send(4, 0, 1, 1)
    zstep(3)
    chunk(3, 5)
    rs_send(3, 1, 1, 0)
    rs_send(5, 1, 0, 1)
    rs_add(3, 0, 0, 0)
    rs_send(3, 1, 0, 0)
    rs_add(5, 0, 1, 1)
    rs_send(5, 1, 1, 1)
    chunk(2, 6)

    zfar = pror.at[yl, lax.rem(z + 4, 8)]
    arrived(zfar.at[PART[0]], Z_ID + 3)
    arrived(zfar.at[PART[1]], Z_ID + 7)
    send(zfar, zfar, PY_ID + 7, ynear)

    for half_r, half_l in ((1, 0), (0, 1)):
        rs_add(2, 1, half_r, 0)
        rs_send(2, 2, half_r, 0)
        rs_add(6, 1, half_l, 1)
        rs_send(6, 2, half_l, 1)
    chunk(1, 7)

    def own_t(s, carry):
        build_t(yl, s)
        return carry

    for half_r, half_l in ((1, 0), (0, 1)):
        rs_add(1, 2, half_r, 0)
        rs_send(1, 3, half_r, 0)
        rs_add(7, 2, half_l, 1)
        rs_send(7, 3, half_l, 1)
    lax.fori_loop(0, 8, own_t, 0)

    near = [pror.at[1 - yl, z]]
    for step in (1, 2, 3):
        near += [pror.at[1 - yl, lax.rem(z + 8 - step, 8)], pror.at[1 - yl, lax.rem(z + step, 8)]]
    near.append(pror.at[1 - yl, lax.rem(z + 4, 8)])
    for n, ref in enumerate(near):
        arrived(ref, PY_ID + n)

    def near_t(s, carry):
        build_t(1 - yl, s)
        return carry

    lax.fori_loop(0, 8, near_t, 0)

    for half in (0, 1):
        rs_add(0, 3, half, 0)
        rs_add(0, 3, half, 1)
        rows = pl.ds(*HALF[half])
        hi, lo = split(q[0, rows, :])
        pcat[rows, pl.ds(0, 128)] = hi
        pcat[rows, pl.ds(128, 128)] = lo

    def coarse_part(gc, gx):
        v = dot(pthi[gc, gx], pcat[...])
        v = v[:, :128] + v[:, 128:] + dot(ptlo[gc, gx], pcat[:, :128])
        cpart[gc, gx, 0] = v[:128]
        cpart[gc, gx, 1] = v[128:]

    def to_other(gx, n):
        coarse_part(1 - core, gx)
        send(cpart.at[1 - core, gx], crecv.at[gx], CC_ID + n, other)

    def from_core(gx, n):
        coarse_part(core, gx)
        arrived(crecv.at[gx], CC_ID + n)
        cpart[core, gx] = cpart[core, gx] + crecv[gx]

    x2 = lax.rem(x + 2, 4)
    xp, xm = lax.rem(x + 1, 4), lax.rem(x + 3, 4)
    cp = cpart.at[core]
    to_other(x2, 0)
    to_other(xp, 1)
    from_core(x2, 0)
    top_bot = (pl.ds(0, 64), pl.ds(64, 64))
    for h, rows in enumerate(top_bot):
        send(cp.at[x2, 0, rows], xr0.at[rows], CX_ID + h, xright)
        send(cp.at[x2, 1, rows], xl0.at[rows], CX_ID + 2 + h, xleft)
    to_other(xm, 2)
    from_core(xp, 1)
    to_other(x, 3)
    from_core(xm, 2)
    for h, rows in enumerate(top_bot):
        arrived(xr0.at[rows], CX_ID + h)
        cpart[core, xp, 0, rows] = cpart[core, xp, 0, rows] + xr0[rows]
        send(cp.at[xp, :, rows], xr1.at[:, rows], CX_ID + 4 + h, xright)
        arrived(xl0.at[rows], CX_ID + 2 + h)
        cpart[core, xm, 1, rows] = cpart[core, xm, 1, rows] + xl0[rows]
        send(cp.at[xm, :, rows], xl1.at[:, rows], CX_ID + 6 + h, xleft)
    from_core(x, 3)
    for i in range(8):
        for h in range(2):
            v = q[0, pl.ds(h * 8 + i, 32, stride=16), :]
            prod_ref[i, 0, pl.ds(h * 32, 32), :] = v[:, :64]
            prod_ref[i, 1, pl.ds(h * 32, 32), :] = v[:, 64:]
    put = pltpu.make_async_copy(prod_ref, prod_hbm, lsem.at[3])
    put.start()
    for h, rows in enumerate(top_bot):
        arrived(xr1.at[:, rows], CX_ID + 4 + h)
        arrived(xl1.at[:, rows], CX_ID + 6 + h)
        cpart[core, x, 1 - yh, rows] = cpart[core, x, 1 - yh, rows] + xr1[1 - yh, rows] + xl1[1 - yh, rows]
        send(cp.at[x, 1 - yh, rows], yrecv.at[rows], CY_ID + h, yfar)
    for h, rows in enumerate(top_bot):
        total = cpart[core, x, yh, rows] + xr1[yh, rows] + xl1[yh, rows]
        arrived(yrecv.at[rows], CY_ID + h)
        total = total + yrecv[rows]
        for b in range(2):
            coarse_ref[h, b] = total[:, b * 64 : b * 64 + 64]

    u = panel.at[0, 0]
    zu = pror.at[0, 0]
    for p in range(2):
        part = u.at[PART[p]]

        @pl.when(jnp.logical_not(own_across))
        def _():
            sent(part, T_ID + p)

        sent(part, Y_ID + p)
        for k in (X_ID, X_ID + 6):
            sent(part, k + p)
            sent(part, k + 2 + p)
            sent(part, k + 4 + p)
    put.wait()
    sent(meta, M_ID)
    for n in range(4):
        sent(alist.at[pl.ds(0, 8)], A_ID + n)
    for n in range(8):
        sent(u, CORE_ID + n)
        sent(zu, PY_ID + n)
    for n in range(3):
        sent(zu, Z_ID + n)
        sent(zu, Z_ID + 4 + n)
    sent(zu.at[PART[0]], Z_ID + 3)
    sent(zu.at[PART[1]], Z_ID + 7)
    piece = q.at[0, pl.ds(0, 256)]
    sent(piece, rs_id(0, 0, 0))
    sent(piece, rs_id(0, 1, 1))
    for step in (1, 2, 3):
        for half in (0, 1):
            for way in (0, 1):
                sent(piece, rs_id(step, half, way))
    for n in range(4):
        sent(crecv.at[0], CC_ID + n)
    for h, rows in enumerate(top_bot):
        sent(xr0.at[rows], CX_ID + h)
        sent(xl0.at[rows], CX_ID + 2 + h)
        sent(xr1.at[:, rows], CX_ID + 4 + h)
        sent(xl1.at[:, rows], CX_ID + 6 + h)
        sent(yrecv.at[rows], CY_ID + h)


def shards(op_tiles, op_rows, op_cols, op_count, pro_tiles, pro_cols, pro_live):
    vmem = pl.BlockSpec(memory_space=pltpu.VMEM)
    smem = pl.BlockSpec(memory_space=pltpu.SMEM)
    anywhere = pl.BlockSpec(memory_space=pl.ANY)
    return pl.pallas_call(
        kernel,
        out_shape=(
            jax.ShapeDtypeStruct((8, 2, 64, 64), F32),
            jax.ShapeDtypeStruct((2, 2, 64, 64), F32),
        ),
        in_specs=[anywhere, vmem, vmem, smem, vmem, smem, smem],
        out_specs=(anywhere, vmem),
        scratch_shapes=[
            pltpu.VMEM((LA, 64, 64), F32),
            pltpu.VMEM((8, 2, 64, 64), F32),
            pltpu.VMEM((8, 128), F32),
            pltpu.VMEM((8, 128), F32),
            pltpu.VMEM((UR, 128), F32),
            pltpu.VMEM((32, LA, 128), F32),
            pltpu.VMEM((32, LA, 128), F32),
            pltpu.VMEM((2, 8, UR, 128), F32),
            pltpu.VMEM((2, 8, UR, 128), F32),
            pltpu.VMEM((2, 512, 512), BF16),
            pltpu.VMEM((2, 512, 512), BF16),
            pltpu.VMEM((2, 512, 256), BF16),
            pltpu.VMEM((2, 512, 256), BF16),
            pltpu.VMEM((8, 512, 128), F32),
            pltpu.VMEM((4, 512, 128), F32),
            pltpu.VMEM((4, 512, 128), F32),
            pltpu.VMEM((2, 4, 256, 512), BF16),
            pltpu.VMEM((2, 4, 256, 512), BF16),
            pltpu.VMEM((512, 256), BF16),
            pltpu.VMEM((2, 4, 2, 128, 128), F32),
            pltpu.VMEM((4, 2, 128, 128), F32),
            pltpu.VMEM((128, 128), F32),
            pltpu.VMEM((128, 128), F32),
            pltpu.VMEM((2, 128, 128), F32),
            pltpu.VMEM((2, 128, 128), F32),
            pltpu.VMEM((128, 128), F32),
            pltpu.SemaphoreType.DMA((N_ID,)),
            pltpu.SemaphoreType.DMA((N_ID,)),
            pltpu.SemaphoreType.DMA((4,)),
        ],
        compiler_params=pltpu.CompilerParams(
            collective_id=0, has_side_effects=True, vmem_limit_bytes=60 * 1024 * 1024
        ),
    )(
        op_tiles.reshape(32, 64, 64), op_rows.T, op_cols.T, op_count,
        pro_tiles.reshape(8, 64, 64), pro_cols.T, pro_live.T,
    )


def solution(mesh):
    return jax.shard_map(
        shards,
        mesh=mesh,
        in_specs=(
            P("row", "col", None, None),
            P("row", "col"),
            P("row", "col"),
            P("row", "col"),
            P("row", "col", None, None),
            P("row", "col"),
            P("row", "col"),
        ),
        out_specs=(P("row", "col", None, None), P("row", "col", None, None)),
        check_vma=False,
    )
```

```python
import functools

import jax
import jax.numpy as jnp
from jax import lax
from jax.experimental import pallas as pl
from jax.experimental.pallas import tpu as pltpu
from jax.sharding import PartitionSpec as P

MESH = pl.DeviceIdType.MESH
F32, BF16 = jnp.float32, jnp.bfloat16
UR = 264
UH = 136
LA = 32
HALF = ((0, 256), (256, 256))
PART = (pl.ds(0, UH), pl.ds(UH, UR - UH))

M_ID = 0
A_ID = 1
T_ID = 5
Y_ID = 7
X_ID = 9
CORE_ID = 21
Z_ID = 29
PY_ID = 37
RS_ID = 45
CC_ID = 61
CX_ID = 65
CY_ID = 73
N_ID = 75


def split(v):
    hi = v.astype(BF16)
    return hi, (v - hi.astype(F32)).astype(BF16)


def pack(tile):
    return jnp.concatenate([tile[:32], tile[32:]], axis=1)


def kernel(
    op_hbm, rows_ref, cols_ref, count_ref, pro_ref, pcols_ref, plive_ref,
    prod_hbm, coarse_ref,
    op_ref, prod_ref, meta, mnear,
    unit, alist, anear, panel, pror, ahi, alo, rhi, rlo, q, rsr, rsl, pthi, ptlo, pcat,
    cpart, crecv, xr0, xl0, xr1, xl1, yrecv,
    ssem, rsem, lsem,
):
    r = lax.axis_index("row")
    c = lax.axis_index("col")
    yh, x, core = r // 8, lax.rem(r // 2, 4), lax.rem(r, 2)
    yl, z = c // 8, lax.rem(c, 8)

    def rowdev(yh_, x_, core_):
        return ((yh_ * 4 + x_) * 2 + core_, c)

    ynear = (r, (1 - yl) * 8 + z)
    zright, zleft = (r, yl * 8 + lax.rem(z + 1, 8)), (r, yl * 8 + lax.rem(z + 7, 8))
    xright, xleft = rowdev(yh, lax.rem(x + 1, 4), core), rowdev(yh, lax.rem(x + 3, 4), core)
    yfar = rowdev(1 - yh, x, core)
    other = rowdev(yh, x, 1 - core)
    turn = 8 - z // 2 - 2 * lax.rem(z, 2)
    s0 = 4 * core + lax.rem(x + turn, 4)
    plane = 2 * x + core
    across = rowdev(yh, lax.rem(z + x + 2 * core, 4), z // 4)[0], yl * 8 + plane
    source = rowdev(yh, z // 2, lax.rem(z, 2))[0], yl * 8 + s0
    own_across = jnp.logical_and(s0 == z, plane == z)

    def send(src, dst, k, dev):
        pltpu.make_async_remote_copy(
            src_ref=src, dst_ref=dst, send_sem=ssem.at[k], recv_sem=rsem.at[k], device_id=dev, device_id_type=MESH
        ).start()

    def arrived(dst, k):
        pltpu.make_async_remote_copy(
            src_ref=dst, dst_ref=dst, send_sem=ssem.at[k], recv_sem=rsem.at[k], device_id=ynear, device_id_type=MESH
        ).wait_recv()

    def sent(src, k):
        pltpu.make_async_remote_copy(
            src_ref=src, dst_ref=src, send_sem=ssem.at[k], recv_sem=rsem.at[k], device_id=ynear, device_id_type=MESH
        ).wait_send()

    fetch = pltpu.make_async_copy(op_hbm, op_ref, lsem.at[2])
    fetch.start()
    barrier = pltpu.get_barrier_semaphore()
    for dev in (ynear, zright, zleft, xright, xleft, yfar, other):
        pl.semaphore_signal(barrier, inc=1, device_id=dev, device_id_type=MESH)

    @pl.when(jnp.logical_not(own_across))
    def _():
        pl.semaphore_signal(barrier, inc=1, device_id=across, device_id_type=MESH)
        pl.semaphore_signal(barrier, inc=1, device_id=source, device_id_type=MESH)

    for k in range(8):
        live = plive_ref[0, k].astype(F32)
        unit[pl.ds(k * 32, 32), :] = pack(pro_ref[k]) * live
        unit[pl.ds(256 + k, 1), :] = jnp.full((1, 128), pcols_ref[0, k].astype(F32))

    pl.semaphore_wait(barrier, jnp.where(own_across, 7, 9))

    @pl.when(own_across)
    def _():
        pltpu.make_async_copy(unit, panel.at[yh, z], lsem.at[0]).start()

    @pl.when(jnp.logical_not(own_across))
    def _():
        for p in range(2):
            send(unit.at[PART[p]], panel.at[yh, z].at[PART[p]], T_ID + p, across)

    keep = pltpu.make_async_copy(unit, pror.at[yl, z], lsem.at[1])
    keep.start()

    pos = rows_ref[...] * 8 + cols_ref[...]
    live_slot = lax.broadcasted_iota(jnp.int32, (1, LA), 1) < count_ref[0, 0]
    pos = jnp.where(live_slot, pos, -1).astype(F32)
    meta[...] = jnp.zeros((8, 128), F32)
    meta[pl.ds(0, 1), pl.ds(0, LA)] = pos
    meta[pl.ds(0, 1), pl.ds(LA, LA)] = pos
    send(meta, mnear, M_ID, ynear)
    fetch.wait()

    def pack_piece(n):
        def slot(t, carry):
            a = op_ref[t, pl.ds(n * 8, 8), :]
            b = op_ref[t, pl.ds(32 + n * 8, 8), :]
            alist[pl.ds(n * 8, 8), t, :] = jnp.concatenate([a, b], axis=1)
            return carry

        lax.fori_loop(0, LA, slot, 0, unroll=8)

    def send_piece(n):
        at = pl.ds(n * 8, 8)
        send(alist.at[at], anear.at[at], A_ID + n, ynear)

    for n in range(4):
        pack_piece(n)
        if n < 2:
            send_piece(n)

    left32 = lax.broadcasted_iota(jnp.int32, (32, 128), 1) < 64
    left8 = lax.broadcasted_iota(jnp.int32, (8, 128), 1) < 64
    place = lax.broadcasted_iota(jnp.int32, (64, 2 * LA), 0)
    place = (lax.rem(place, 8) * 8 + place // 8).astype(F32)

    def dot(a, b):
        return lax.dot_general(a, b, (((1,), (0,)), ((), ())), preferred_element_type=F32)

    def build_a(src, which, at, n):
        hot = (which[pl.ds(0, 1), pl.ds(0, 2 * LA)] == place).astype(F32).astype(BF16)

        def row(step, carry):
            rho = n * 8 + step * 2
            h0, l0 = split(src[rho])
            h1, l1 = split(src[rho + 1])
            both = jnp.concatenate(
                [jnp.concatenate([h0, l0], axis=0), jnp.concatenate([h1, l1], axis=0)], axis=1
            )
            tiles = dot(hot, both)
            for e in range(2):
                t = tiles[:, e * 128 : e * 128 + 128]
                for m in range(4):
                    even, odd = t[m * 16 : m * 16 + 8], t[m * 16 + 8 : m * 16 + 16]
                    top = jnp.where(left8, even, pltpu.roll(odd, 64, 1))
                    bot = jnp.where(left8, pltpu.roll(even, 64, 1), odd)
                    hi, lo = split(jnp.concatenate([top, bot], axis=0))
                    at_rows = pl.ds(pl.multiple_of((rho + e) * 16, 16), 16)
                    ahi[at, at_rows, pl.ds(m * 128, 128)] = hi
                    alo[at, at_rows, pl.ds(m * 128, 128)] = lo
            return carry

        lax.fori_loop(0, 4, row, 0)

    def dense(ref, b, s, k):
        tile = ref[b, s, pl.ds(k * 32, 32), :]
        col = ref[b, s, pl.ds(256 + k, 1), :]
        turned = pltpu.roll(tile, 64, 1)
        a, bb = 1.0 - col, col
        top = jnp.where(left32, tile * a, turned * bb)
        bot = jnp.where(left32, turned * a, tile * bb)
        return top, bot

    zu = pror.at[yl, z]
    send(unit, zu, Z_ID, zright)
    send(unit, zu, Z_ID + 4, zleft)
    build_a(alist, meta, yl, 0)

    def ring(off):
        return 4 * core + lax.rem(x + turn + off, 4)

    mine, theirs = yh, 1 - yh
    sl, sr, sf = ring(3), ring(1), ring(2)

    def spread(b, k, p):
        u = panel.at[b, s0].at[PART[p]]
        send(u, u, k + p, xright)
        send(u, u, k + 2 + p, xleft)

    def onward(b, k):
        u = panel.at[b, sl].at[PART[0]]
        arrived(u, k)
        send(u, u, k + 4, xright)
        u = panel.at[b, sr].at[PART[1]]
        arrived(u, k + 3)
        send(u, u, k + 5, xleft)

    def beside(b, k, kc):
        u = panel.at[b, sl]
        arrived(u.at[PART[1]], k + 1)
        send(u, u, kc + 1, other)
        u = panel.at[b, sr]
        arrived(u.at[PART[0]], k + 2)
        send(u, u, kc + 2, other)

    def far(b, k, kc):
        u = panel.at[b, sf]
        arrived(u.at[PART[0]], k + 4)
        arrived(u.at[PART[1]], k + 5)
        send(u, u, kc + 3, other)

    def zstep(step):
        got_r = pror.at[yl, lax.rem(z + 8 - step, 8)]
        got_l = pror.at[yl, lax.rem(z + step, 8)]
        arrived(got_r, Z_ID + step - 1)
        arrived(got_l, Z_ID + 4 + step - 1)
        if step < 3:
            send(got_r, got_r, Z_ID + step, zright)
            send(got_l, got_l, Z_ID + 4 + step, zleft)
        else:
            send(got_r.at[PART[0]], got_r.at[PART[0]], Z_ID + 3, zright)
            send(got_l.at[PART[1]], got_l.at[PART[1]], Z_ID + 7, zleft)
        send(got_r, got_r, PY_ID + 2 * step - 1, ynear)
        send(got_l, got_l, PY_ID + 2 * step, ynear)

    u = panel.at[mine, s0]

    @pl.when(own_across)
    def _():
        pltpu.make_async_copy(unit, panel.at[yh, z], lsem.at[0]).wait()

    for p in range(2):
        @pl.when(jnp.logical_not(own_across))
        def _():
            arrived(u.at[PART[p]], T_ID + p)

        send(u.at[PART[p]], u.at[PART[p]], Y_ID + p, yfar)
        spread(mine, X_ID, p)
    send_piece(2)
    send_piece(3)
    send(u, u, CORE_ID, other)
    keep.wait()
    send(zu, zu, PY_ID, ynear)
    zstep(1)
    build_a(alist, meta, yl, 1)
    onward(mine, X_ID)
    build_a(alist, meta, yl, 2)
    u = panel.at[theirs, s0]
    for p in range(2):
        arrived(u.at[PART[p]], Y_ID + p)
        spread(theirs, X_ID + 6, p)
    send(u, u, CORE_ID + 4, other)
    beside(mine, X_ID, CORE_ID)
    build_a(alist, meta, yl, 3)
    zstep(2)
    onward(theirs, X_ID + 6)
    far(mine, X_ID, CORE_ID)
    arrived(mnear, M_ID)
    for n in range(2):
        arrived(anear.at[pl.ds(n * 8, 8)], A_ID + n)
        build_a(anear, mnear, 1 - yl, n)
    beside(theirs, X_ID + 6, CORE_ID + 4)
    zstep(3)
    far(theirs, X_ID + 6, CORE_ID + 4)
    for n in range(2, 4):
        arrived(anear.at[pl.ds(n * 8, 8)], A_ID + n)
        build_a(anear, mnear, 1 - yl, n)
    for n in range(8):
        s = 4 * (1 - core) + lax.rem(x + turn + (0, 3, 1, 2)[n % 4], 4)
        arrived(panel.at[(mine, theirs)[n // 4], s], CORE_ID + n)

    def build_r(d, at):
        s = lax.rem(z + d, 8)

        def block(b, carry):
            for k in range(8):
                for off, v in zip((0, 32), dense(panel, b, s, k)):
                    hi, lo = split(v)
                    rhi[b, pl.ds(k * 64 + off, 32), pl.ds(at * 128, 128)] = hi
                    rlo[b, pl.ds(k * 64 + off, 32), pl.ds(at * 128, 128)] = lo
            return carry

        lax.fori_loop(0, 2, block, 0)

    def chunk_one(d):
        build_r(d, 0)

        def part(m, carry):
            rows = pl.ds(pl.multiple_of(m * 256, 256), 256)
            acc = jnp.zeros((256, 128), F32)
            for b in range(2):
                h, l = ahi[b, rows, :], alo[b, rows, :]
                rh = rhi[b, :, pl.ds(0, 128)]
                acc = acc + dot(h, rh) + dot(h, rlo[b, :, pl.ds(0, 128)]) + dot(l, rh)
            q[d, rows, :] = acc
            return carry

        lax.fori_loop(0, 2, part, 0)

    def chunk(d0, d1):
        build_r(d0, 0)
        build_r(d1, 1)

        def part(m, carry):
            rows = pl.ds(pl.multiple_of(m * 256, 256), 256)
            acc = jnp.zeros((256, 256), F32)
            for b in range(2):
                h, l = ahi[b, rows, :], alo[b, rows, :]
                acc = acc + dot(h, rhi[b]) + dot(h, rlo[b]) + dot(l, rhi[b])
            q[d0, rows, :] = acc[:, :128]
            q[d1, rows, :] = acc[:, 128:]
            return carry

        lax.fori_loop(0, 2, part, 0)

    def rs_id(step, half, way):
        return RS_ID + (step * 2 + half) * 2 + way

    def rs_send(d, step, half, way):
        rows = pl.ds(*HALF[half])
        buf = (rsr, rsl)[way]
        send(q.at[d, rows], buf.at[step, rows], rs_id(step, half, way), (zright, zleft)[way])

    def rs_add(d, step, half, way):
        rows = pl.ds(*HALF[half])
        buf = (rsr, rsl)[way]
        arrived(buf.at[step, rows], rs_id(step, half, way))
        q[d, rows, :] = q[d, rows, :] + buf[step, rows, :]

    def build_t(b, s):
        flag = pror[b, s, pl.ds(256, 8), :]
        for m in range(4):
            parts = []
            for rho in range(8 * m, 8 * m + 8):
                tile = pror[b, s, pl.ds(rho, 8, stride=32), :]
                turned = pltpu.roll(tile, 64, 1)
                parts.append(jnp.where(left8, tile * (1.0 - flag), turned * flag))
                parts.append(jnp.where(left8, turned * (1.0 - flag), tile * flag))
            hi, lo = split(jnp.concatenate(parts, axis=0).T)
            g = b * 8 + s
            rows = pl.ds(pl.multiple_of(g // 8 * 128, 128), 128)
            pthi[lax.rem(g, 2), lax.rem(g // 2, 4), rows, pl.ds(m * 128, 128)] = hi
            ptlo[lax.rem(g, 2), lax.rem(g // 2, 4), rows, pl.ds(m * 128, 128)] = lo

    chunk_one(4)
    rs_send(4, 0, 0, 0)
    rs_send(4, 0, 1, 1)
    chunk(3, 5)
    rs_send(3, 1, 1, 0)
    rs_send(5, 1, 0, 1)
    rs_add(3, 0, 0, 0)
    rs_send(3, 1, 0, 0)
    rs_add(5, 0, 1, 1)
    rs_send(5, 1, 1, 1)
    zfar = pror.at[yl, lax.rem(z + 4, 8)]
    arrived(zfar.at[PART[0]], Z_ID + 3)
    arrived(zfar.at[PART[1]], Z_ID + 7)
    send(zfar, zfar, PY_ID + 7, ynear)

    chunk(2, 6)

    for half_r, half_l in ((1, 0), (0, 1)):
        rs_add(2, 1, half_r, 0)
        rs_send(2, 2, half_r, 0)
        rs_add(6, 1, half_l, 1)
        rs_send(6, 2, half_l, 1)
    chunk(1, 7)

    def own_t(s, carry):
        build_t(yl, s)
        return carry

    for half_r, half_l in ((1, 0), (0, 1)):
        rs_add(1, 2, half_r, 0)
        rs_send(1, 3, half_r, 0)
        rs_add(7, 2, half_l, 1)
        rs_send(7, 3, half_l, 1)
    chunk_one(0)
    lax.fori_loop(0, 8, own_t, 0)

    near = [pror.at[1 - yl, z]]
    for step in (1, 2, 3):
        near += [pror.at[1 - yl, lax.rem(z + 8 - step, 8)], pror.at[1 - yl, lax.rem(z + step, 8)]]
    near.append(pror.at[1 - yl, lax.rem(z + 4, 8)])
    for n, ref in enumerate(near):
        arrived(ref, PY_ID + n)

    def near_t(s, carry):
        build_t(1 - yl, s)
        return carry

    lax.fori_loop(0, 8, near_t, 0)

    for half in (0, 1):
        rs_add(0, 3, half, 0)
        rs_add(0, 3, half, 1)
        rows = pl.ds(*HALF[half])
        hi, lo = split(q[0, rows, :])
        pcat[rows, pl.ds(0, 128)] = hi
        pcat[rows, pl.ds(128, 128)] = lo

    def coarse_part(gc, gx):
        v = dot(pthi[gc, gx], pcat[...])
        v = v[:, :128] + v[:, 128:] + dot(ptlo[gc, gx], pcat[:, :128])
        cpart[gc, gx, 0] = v[:128]
        cpart[gc, gx, 1] = v[128:]

    def to_other(gx, n):
        coarse_part(1 - core, gx)
        send(cpart.at[1 - core, gx], crecv.at[gx], CC_ID + n, other)

    def from_core(gx, n):
        coarse_part(core, gx)
        arrived(crecv.at[gx], CC_ID + n)
        cpart[core, gx] = cpart[core, gx] + crecv[gx]

    x2 = lax.rem(x + 2, 4)
    xp, xm = lax.rem(x + 1, 4), lax.rem(x + 3, 4)
    cp = cpart.at[core]
    to_other(x2, 0)
    to_other(xp, 1)
    from_core(x2, 0)
    top_bot = (pl.ds(0, 64), pl.ds(64, 64))
    for h, rows in enumerate(top_bot):
        send(cp.at[x2, 0, rows], xr0.at[rows], CX_ID + h, xright)
        send(cp.at[x2, 1, rows], xl0.at[rows], CX_ID + 2 + h, xleft)
    to_other(xm, 2)
    from_core(xp, 1)
    to_other(x, 3)
    from_core(xm, 2)
    for h, rows in enumerate(top_bot):
        arrived(xr0.at[rows], CX_ID + h)
        cpart[core, xp, 0, rows] = cpart[core, xp, 0, rows] + xr0[rows]
        send(cp.at[xp, :, rows], xr1.at[:, rows], CX_ID + 4 + h, xright)
        arrived(xl0.at[rows], CX_ID + 2 + h)
        cpart[core, xm, 1, rows] = cpart[core, xm, 1, rows] + xl0[rows]
        send(cp.at[xm, :, rows], xl1.at[:, rows], CX_ID + 6 + h, xleft)
    from_core(x, 3)
    for i in range(8):
        for h in range(2):
            v = q[0, pl.ds(h * 8 + i, 32, stride=16), :]
            prod_ref[i, 0, pl.ds(h * 32, 32), :] = v[:, :64]
            prod_ref[i, 1, pl.ds(h * 32, 32), :] = v[:, 64:]
    put = pltpu.make_async_copy(prod_ref, prod_hbm, lsem.at[3])
    put.start()
    for h, rows in enumerate(top_bot):
        arrived(xr1.at[:, rows], CX_ID + 4 + h)
        arrived(xl1.at[:, rows], CX_ID + 6 + h)
        cpart[core, x, 1 - yh, rows] = cpart[core, x, 1 - yh, rows] + xr1[1 - yh, rows] + xl1[1 - yh, rows]
        send(cp.at[x, 1 - yh, rows], yrecv.at[rows], CY_ID + h, yfar)
    for h, rows in enumerate(top_bot):
        total = cpart[core, x, yh, rows] + xr1[yh, rows] + xl1[yh, rows]
        arrived(yrecv.at[rows], CY_ID + h)
        total = total + yrecv[rows]
        for b in range(2):
            coarse_ref[h, b] = total[:, b * 64 : b * 64 + 64]

    u = panel.at[0, 0]
    zu = pror.at[0, 0]
    for p in range(2):
        part = u.at[PART[p]]

        @pl.when(jnp.logical_not(own_across))
        def _():
            sent(part, T_ID + p)

        sent(part, Y_ID + p)
        for k in (X_ID, X_ID + 6):
            sent(part, k + p)
            sent(part, k + 2 + p)
            sent(part, k + 4 + p)
    put.wait()
    sent(meta, M_ID)
    for n in range(4):
        sent(alist.at[pl.ds(0, 8)], A_ID + n)
    for n in range(8):
        sent(u, CORE_ID + n)
        sent(zu, PY_ID + n)
    for n in range(3):
        sent(zu, Z_ID + n)
        sent(zu, Z_ID + 4 + n)
    sent(zu.at[PART[0]], Z_ID + 3)
    sent(zu.at[PART[1]], Z_ID + 7)
    piece = q.at[0, pl.ds(0, 256)]
    sent(piece, rs_id(0, 0, 0))
    sent(piece, rs_id(0, 1, 1))
    for step in (1, 2, 3):
        for half in (0, 1):
            for way in (0, 1):
                sent(piece, rs_id(step, half, way))
    for n in range(4):
        sent(crecv.at[0], CC_ID + n)
    for h, rows in enumerate(top_bot):
        sent(xr0.at[rows], CX_ID + h)
        sent(xl0.at[rows], CX_ID + 2 + h)
        sent(xr1.at[:, rows], CX_ID + 4 + h)
        sent(xl1.at[:, rows], CX_ID + 6 + h)
        sent(yrecv.at[rows], CY_ID + h)


def shards(op_tiles, op_rows, op_cols, op_count, pro_tiles, pro_cols, pro_live):
    vmem = pl.BlockSpec(memory_space=pltpu.VMEM)
    smem = pl.BlockSpec(memory_space=pltpu.SMEM)
    anywhere = pl.BlockSpec(memory_space=pl.ANY)
    return pl.pallas_call(
        kernel,
        out_shape=(
            jax.ShapeDtypeStruct((8, 2, 64, 64), F32),
            jax.ShapeDtypeStruct((2, 2, 64, 64), F32),
        ),
        in_specs=[anywhere, vmem, vmem, smem, vmem, smem, smem],
        out_specs=(anywhere, vmem),
        scratch_shapes=[
            pltpu.VMEM((LA, 64, 64), F32),
            pltpu.VMEM((8, 2, 64, 64), F32),
            pltpu.VMEM((8, 128), F32),
            pltpu.VMEM((8, 128), F32),
            pltpu.VMEM((UR, 128), F32),
            pltpu.VMEM((32, LA, 128), F32),
            pltpu.VMEM((32, LA, 128), F32),
            pltpu.VMEM((2, 8, UR, 128), F32),
            pltpu.VMEM((2, 8, UR, 128), F32),
            pltpu.VMEM((2, 512, 512), BF16),
            pltpu.VMEM((2, 512, 512), BF16),
            pltpu.VMEM((2, 512, 256), BF16),
            pltpu.VMEM((2, 512, 256), BF16),
            pltpu.VMEM((8, 512, 128), F32),
            pltpu.VMEM((4, 512, 128), F32),
            pltpu.VMEM((4, 512, 128), F32),
            pltpu.VMEM((2, 4, 256, 512), BF16),
            pltpu.VMEM((2, 4, 256, 512), BF16),
            pltpu.VMEM((512, 256), BF16),
            pltpu.VMEM((2, 4, 2, 128, 128), F32),
            pltpu.VMEM((4, 2, 128, 128), F32),
            pltpu.VMEM((128, 128), F32),
            pltpu.VMEM((128, 128), F32),
            pltpu.VMEM((2, 128, 128), F32),
            pltpu.VMEM((2, 128, 128), F32),
            pltpu.VMEM((128, 128), F32),
            pltpu.SemaphoreType.DMA((N_ID,)),
            pltpu.SemaphoreType.DMA((N_ID,)),
            pltpu.SemaphoreType.DMA((4,)),
        ],
        compiler_params=pltpu.CompilerParams(
            collective_id=0, has_side_effects=True, vmem_limit_bytes=60 * 1024 * 1024
        ),
    )(
        op_tiles.reshape(32, 64, 64), op_rows.T, op_cols.T, op_count,
        pro_tiles.reshape(8, 64, 64), pro_cols.T, pro_live.T,
    )


def solution(mesh):
    return jax.shard_map(
        shards,
        mesh=mesh,
        in_specs=(
            P("row", "col", None, None),
            P("row", "col"),
            P("row", "col"),
            P("row", "col"),
            P("row", "col", None, None),
            P("row", "col"),
            P("row", "col"),
        ),
        out_specs=(P("row", "col", None, None), P("row", "col", None, None)),
        check_vma=False,
    )
```

```python
import functools

import jax
import jax.numpy as jnp
from jax import lax
from jax.experimental import pallas as pl
from jax.experimental.pallas import tpu as pltpu
from jax.sharding import PartitionSpec as P

MESH = pl.DeviceIdType.MESH
F32, BF16 = jnp.float32, jnp.bfloat16
UR = 264
UH = 136
LA = 32
HALF = ((0, 256), (256, 256))
PART = (pl.ds(0, UH), pl.ds(UH, UR - UH))

M_ID = 0
A_ID = 1
T_ID = 5
Y_ID = 7
X_ID = 9
CORE_ID = 21
Z_ID = 29
PY_ID = 37
RS_ID = 45
CC_ID = 61
CX_ID = 65
CY_ID = 73
N_ID = 75


def split(v):
    hi = v.astype(BF16)
    return hi, (v - hi.astype(F32)).astype(BF16)


def pack(tile):
    return jnp.concatenate([tile[:32], tile[32:]], axis=1)


def kernel(
    op_hbm, rows_ref, cols_ref, count_ref, pro_ref, pcols_ref, plive_ref,
    prod_hbm, coarse_ref,
    op_ref, prod_ref, meta, mnear,
    unit, alist, anear, panel, pror, ahi, alo, rhi, rlo, q, rsr, rsl, pthi, ptlo, pcat,
    cpart, crecv, xr0, xl0, xr1, xl1, yrecv,
    ssem, rsem, lsem,
):
    r = lax.axis_index("row")
    c = lax.axis_index("col")
    yh, x, core = r // 8, lax.rem(r // 2, 4), lax.rem(r, 2)
    yl, z = c // 8, lax.rem(c, 8)

    def rowdev(yh_, x_, core_):
        return ((yh_ * 4 + x_) * 2 + core_, c)

    ynear = (r, (1 - yl) * 8 + z)
    zright, zleft = (r, yl * 8 + lax.rem(z + 1, 8)), (r, yl * 8 + lax.rem(z + 7, 8))
    xright, xleft = rowdev(yh, lax.rem(x + 1, 4), core), rowdev(yh, lax.rem(x + 3, 4), core)
    yfar = rowdev(1 - yh, x, core)
    other = rowdev(yh, x, 1 - core)
    turn = 8 - z // 2 - 2 * lax.rem(z, 2)
    s0 = 4 * core + lax.rem(x + turn, 4)
    plane = 2 * x + core
    across = rowdev(yh, lax.rem(z + x + 2 * core, 4), z // 4)[0], yl * 8 + plane
    source = rowdev(yh, z // 2, lax.rem(z, 2))[0], yl * 8 + s0
    own_across = jnp.logical_and(s0 == z, plane == z)

    def send(src, dst, k, dev):
        pltpu.make_async_remote_copy(
            src_ref=src, dst_ref=dst, send_sem=ssem.at[k], recv_sem=rsem.at[k], device_id=dev, device_id_type=MESH
        ).start()

    def arrived(dst, k):
        pltpu.make_async_remote_copy(
            src_ref=dst, dst_ref=dst, send_sem=ssem.at[k], recv_sem=rsem.at[k], device_id=ynear, device_id_type=MESH
        ).wait_recv()

    def sent(src, k):
        pltpu.make_async_remote_copy(
            src_ref=src, dst_ref=src, send_sem=ssem.at[k], recv_sem=rsem.at[k], device_id=ynear, device_id_type=MESH
        ).wait_send()

    fetch = pltpu.make_async_copy(op_hbm, op_ref, lsem.at[2])
    fetch.start()
    barrier = pltpu.get_barrier_semaphore()
    for dev in (ynear, zright, zleft, xright, xleft, yfar, other):
        pl.semaphore_signal(barrier, inc=1, device_id=dev, device_id_type=MESH)

    @pl.when(jnp.logical_not(own_across))
    def _():
        pl.semaphore_signal(barrier, inc=1, device_id=across, device_id_type=MESH)
        pl.semaphore_signal(barrier, inc=1, device_id=source, device_id_type=MESH)

    for k in range(8):
        live = plive_ref[0, k].astype(F32)
        unit[pl.ds(k * 32, 32), :] = pack(pro_ref[k]) * live
        unit[pl.ds(256 + k, 1), :] = jnp.full((1, 128), pcols_ref[0, k].astype(F32))

    pl.semaphore_wait(barrier, jnp.where(own_across, 7, 9))

    @pl.when(own_across)
    def _():
        pltpu.make_async_copy(unit, panel.at[yh, z], lsem.at[0]).start()

    @pl.when(jnp.logical_not(own_across))
    def _():
        for p in range(2):
            send(unit.at[PART[p]], panel.at[yh, z].at[PART[p]], T_ID + p, across)

    keep = pltpu.make_async_copy(unit, pror.at[yl, z], lsem.at[1])
    keep.start()

    pos = rows_ref[...] * 8 + cols_ref[...]
    live_slot = lax.broadcasted_iota(jnp.int32, (1, LA), 1) < count_ref[0, 0]
    pos = jnp.where(live_slot, pos, -1).astype(F32)
    meta[...] = jnp.zeros((8, 128), F32)
    meta[pl.ds(0, 1), pl.ds(0, LA)] = pos
    meta[pl.ds(0, 1), pl.ds(LA, LA)] = pos
    send(meta, mnear, M_ID, ynear)
    fetch.wait()

    def pack_piece(n):
        def slot(t, carry):
            a = op_ref[t, pl.ds(n * 8, 8), :]
            b = op_ref[t, pl.ds(32 + n * 8, 8), :]
            alist[pl.ds(n * 8, 8), t, :] = jnp.concatenate([a, b], axis=1)
            return carry

        lax.fori_loop(0, LA, slot, 0, unroll=8)

    def send_piece(n):
        at = pl.ds(n * 8, 8)
        send(alist.at[at], anear.at[at], A_ID + n, ynear)

    for n in range(4):
        pack_piece(n)
        if n < 2:
            send_piece(n)

    left32 = lax.broadcasted_iota(jnp.int32, (32, 128), 1) < 64
    left8 = lax.broadcasted_iota(jnp.int32, (8, 128), 1) < 64
    place = lax.broadcasted_iota(jnp.int32, (64, 2 * LA), 0)
    place = (lax.rem(place, 8) * 8 + place // 8).astype(F32)

    def dot(a, b):
        return lax.dot_general(a, b, (((1,), (0,)), ((), ())), preferred_element_type=F32)

    def build_a(src, which, at, n):
        hot = (which[pl.ds(0, 1), pl.ds(0, 2 * LA)] == place).astype(F32).astype(BF16)

        def row(step, carry):
            rho = n * 8 + step * 4
            columns = []
            for e in range(4):
                columns.append(jnp.concatenate(split(src[rho + e]), axis=0))
            tiles = dot(hot, jnp.concatenate(columns, axis=1))
            for e in range(4):
                t = tiles[:, e * 128 : e * 128 + 128]
                for m in range(4):
                    even, odd = t[m * 16 : m * 16 + 8], t[m * 16 + 8 : m * 16 + 16]
                    top = jnp.where(left8, even, pltpu.roll(odd, 64, 1))
                    bot = jnp.where(left8, pltpu.roll(even, 64, 1), odd)
                    hi, lo = split(jnp.concatenate([top, bot], axis=0))
                    at_rows = pl.ds(pl.multiple_of((rho + e) * 16, 16), 16)
                    ahi[at, at_rows, pl.ds(m * 128, 128)] = hi
                    alo[at, at_rows, pl.ds(m * 128, 128)] = lo
            return carry

        lax.fori_loop(0, 2, row, 0, unroll=2)

    def dense(ref, b, s, k):
        tile = ref[b, s, pl.ds(k * 32, 32), :]
        col = ref[b, s, pl.ds(256 + k, 1), :]
        turned = pltpu.roll(tile, 64, 1)
        a, bb = 1.0 - col, col
        top = jnp.where(left32, tile * a, turned * bb)
        bot = jnp.where(left32, turned * a, tile * bb)
        return top, bot

    zu = pror.at[yl, z]
    send(unit, zu, Z_ID, zright)
    send(unit, zu, Z_ID + 4, zleft)
    build_a(alist, meta, yl, 0)

    def ring(off):
        return 4 * core + lax.rem(x + turn + off, 4)

    mine, theirs = yh, 1 - yh
    sl, sr, sf = ring(3), ring(1), ring(2)

    def spread(b, k, p):
        u = panel.at[b, s0].at[PART[p]]
        send(u, u, k + p, xright)
        send(u, u, k + 2 + p, xleft)

    def onward(b, k):
        u = panel.at[b, sl].at[PART[0]]
        arrived(u, k)
        send(u, u, k + 4, xright)
        u = panel.at[b, sr].at[PART[1]]
        arrived(u, k + 3)
        send(u, u, k + 5, xleft)

    def beside(b, k, kc):
        u = panel.at[b, sl]
        arrived(u.at[PART[1]], k + 1)
        send(u, u, kc + 1, other)
        u = panel.at[b, sr]
        arrived(u.at[PART[0]], k + 2)
        send(u, u, kc + 2, other)

    def far(b, k, kc):
        u = panel.at[b, sf]
        arrived(u.at[PART[0]], k + 4)
        arrived(u.at[PART[1]], k + 5)
        send(u, u, kc + 3, other)

    def zstep(step):
        got_r = pror.at[yl, lax.rem(z + 8 - step, 8)]
        got_l = pror.at[yl, lax.rem(z + step, 8)]
        arrived(got_r, Z_ID + step - 1)
        arrived(got_l, Z_ID + 4 + step - 1)
        if step < 3:
            send(got_r, got_r, Z_ID + step, zright)
            send(got_l, got_l, Z_ID + 4 + step, zleft)
        else:
            send(got_r.at[PART[0]], got_r.at[PART[0]], Z_ID + 3, zright)
            send(got_l.at[PART[1]], got_l.at[PART[1]], Z_ID + 7, zleft)
        send(got_r, got_r, PY_ID + 2 * step - 1, ynear)
        send(got_l, got_l, PY_ID + 2 * step, ynear)

    u = panel.at[mine, s0]

    @pl.when(own_across)
    def _():
        pltpu.make_async_copy(unit, panel.at[yh, z], lsem.at[0]).wait()

    for p in range(2):
        @pl.when(jnp.logical_not(own_across))
        def _():
            arrived(u.at[PART[p]], T_ID + p)

        send(u.at[PART[p]], u.at[PART[p]], Y_ID + p, yfar)
        spread(mine, X_ID, p)
    send_piece(2)
    send_piece(3)
    send(u, u, CORE_ID, other)
    keep.wait()
    send(zu, zu, PY_ID, ynear)
    zstep(1)
    build_a(alist, meta, yl, 1)
    onward(mine, X_ID)
    build_a(alist, meta, yl, 2)
    u = panel.at[theirs, s0]
    for p in range(2):
        arrived(u.at[PART[p]], Y_ID + p)
        spread(theirs, X_ID + 6, p)
    send(u, u, CORE_ID + 4, other)
    beside(mine, X_ID, CORE_ID)
    build_a(alist, meta, yl, 3)
    zstep(2)
    onward(theirs, X_ID + 6)
    far(mine, X_ID, CORE_ID)
    arrived(mnear, M_ID)
    for n in range(2):
        arrived(anear.at[pl.ds(n * 8, 8)], A_ID + n)
        build_a(anear, mnear, 1 - yl, n)
    beside(theirs, X_ID + 6, CORE_ID + 4)
    zstep(3)
    far(theirs, X_ID + 6, CORE_ID + 4)
    for n in range(2, 4):
        arrived(anear.at[pl.ds(n * 8, 8)], A_ID + n)
        build_a(anear, mnear, 1 - yl, n)
    for n in range(8):
        s = 4 * (1 - core) + lax.rem(x + turn + (0, 3, 1, 2)[n % 4], 4)
        arrived(panel.at[(mine, theirs)[n // 4], s], CORE_ID + n)

    def build_r(d, at):
        s = lax.rem(z + d, 8)

        def block(b, carry):
            for k in range(8):
                for off, v in zip((0, 32), dense(panel, b, s, k)):
                    hi, lo = split(v)
                    rhi[b, pl.ds(k * 64 + off, 32), pl.ds(at * 128, 128)] = hi
                    rlo[b, pl.ds(k * 64 + off, 32), pl.ds(at * 128, 128)] = lo
            return carry

        lax.fori_loop(0, 2, block, 0)

    def chunk_one(d):
        build_r(d, 0)

        def part(m, carry):
            rows = pl.ds(pl.multiple_of(m * 256, 256), 256)
            acc = jnp.zeros((256, 128), F32)
            for b in range(2):
                h, l = ahi[b, rows, :], alo[b, rows, :]
                rh = rhi[b, :, pl.ds(0, 128)]
                acc = acc + dot(h, rh) + dot(h, rlo[b, :, pl.ds(0, 128)]) + dot(l, rh)
            q[d, rows, :] = acc
            return carry

        lax.fori_loop(0, 2, part, 0)

    def chunk(d0, d1):
        build_r(d0, 0)
        build_r(d1, 1)

        def part(m, carry):
            rows = pl.ds(pl.multiple_of(m * 256, 256), 256)
            acc = jnp.zeros((256, 256), F32)
            for b in range(2):
                h, l = ahi[b, rows, :], alo[b, rows, :]
                acc = acc + dot(h, rhi[b]) + dot(h, rlo[b]) + dot(l, rhi[b])
            q[d0, rows, :] = acc[:, :128]
            q[d1, rows, :] = acc[:, 128:]
            return carry

        lax.fori_loop(0, 2, part, 0)

    def rs_id(step, half, way):
        return RS_ID + (step * 2 + half) * 2 + way

    def rs_send(d, step, half, way):
        rows = pl.ds(*HALF[half])
        buf = (rsr, rsl)[way]
        send(q.at[d, rows], buf.at[step, rows], rs_id(step, half, way), (zright, zleft)[way])

    def rs_add(d, step, half, way):
        rows = pl.ds(*HALF[half])
        buf = (rsr, rsl)[way]
        arrived(buf.at[step, rows], rs_id(step, half, way))
        q[d, rows, :] = q[d, rows, :] + buf[step, rows, :]

    def build_t(b, s):
        flag = pror[b, s, pl.ds(256, 8), :]
        for m in range(4):
            parts = []
            for rho in range(8 * m, 8 * m + 8):
                tile = pror[b, s, pl.ds(rho, 8, stride=32), :]
                turned = pltpu.roll(tile, 64, 1)
                parts.append(jnp.where(left8, tile * (1.0 - flag), turned * flag))
                parts.append(jnp.where(left8, turned * (1.0 - flag), tile * flag))
            hi, lo = split(jnp.concatenate(parts, axis=0).T)
            g = b * 8 + s
            rows = pl.ds(pl.multiple_of(g // 8 * 128, 128), 128)
            pthi[lax.rem(g, 2), lax.rem(g // 2, 4), rows, pl.ds(m * 128, 128)] = hi
            ptlo[lax.rem(g, 2), lax.rem(g // 2, 4), rows, pl.ds(m * 128, 128)] = lo

    chunk_one(4)
    rs_send(4, 0, 0, 0)
    rs_send(4, 0, 1, 1)
    chunk(3, 5)
    rs_send(3, 1, 1, 0)
    rs_send(5, 1, 0, 1)
    rs_add(3, 0, 0, 0)
    rs_send(3, 1, 0, 0)
    rs_add(5, 0, 1, 1)
    rs_send(5, 1, 1, 1)
    zfar = pror.at[yl, lax.rem(z + 4, 8)]
    arrived(zfar.at[PART[0]], Z_ID + 3)
    arrived(zfar.at[PART[1]], Z_ID + 7)
    send(zfar, zfar, PY_ID + 7, ynear)

    chunk(2, 6)

    for half_r, half_l in ((1, 0), (0, 1)):
        rs_add(2, 1, half_r, 0)
        rs_send(2, 2, half_r, 0)
        rs_add(6, 1, half_l, 1)
        rs_send(6, 2, half_l, 1)
    chunk(1, 7)

    def own_t(s, carry):
        build_t(yl, s)
        return carry

    for half_r, half_l in ((1, 0), (0, 1)):
        rs_add(1, 2, half_r, 0)
        rs_send(1, 3, half_r, 0)
        rs_add(7, 2, half_l, 1)
        rs_send(7, 3, half_l, 1)
    chunk_one(0)
    lax.fori_loop(0, 8, own_t, 0)

    near = [pror.at[1 - yl, z]]
    for step in (1, 2, 3):
        near += [pror.at[1 - yl, lax.rem(z + 8 - step, 8)], pror.at[1 - yl, lax.rem(z + step, 8)]]
    near.append(pror.at[1 - yl, lax.rem(z + 4, 8)])
    for n, ref in enumerate(near):
        arrived(ref, PY_ID + n)

    def near_t(s, carry):
        build_t(1 - yl, s)
        return carry

    lax.fori_loop(0, 8, near_t, 0)

    for half in (0, 1):
        rs_add(0, 3, half, 0)
        rs_add(0, 3, half, 1)
        rows = pl.ds(*HALF[half])
        hi, lo = split(q[0, rows, :])
        pcat[rows, pl.ds(0, 128)] = hi
        pcat[rows, pl.ds(128, 128)] = lo

    def coarse_part(gc, gx):
        v = dot(pthi[gc, gx], pcat[...])
        v = v[:, :128] + v[:, 128:] + dot(ptlo[gc, gx], pcat[:, :128])
        cpart[gc, gx, 0] = v[:128]
        cpart[gc, gx, 1] = v[128:]

    def to_other(gx, n):
        coarse_part(1 - core, gx)
        send(cpart.at[1 - core, gx], crecv.at[gx], CC_ID + n, other)

    def from_core(gx, n):
        coarse_part(core, gx)
        arrived(crecv.at[gx], CC_ID + n)
        cpart[core, gx] = cpart[core, gx] + crecv[gx]

    x2 = lax.rem(x + 2, 4)
    xp, xm = lax.rem(x + 1, 4), lax.rem(x + 3, 4)
    cp = cpart.at[core]
    to_other(x2, 0)
    to_other(xp, 1)
    from_core(x2, 0)
    top_bot = (pl.ds(0, 64), pl.ds(64, 64))
    for h, rows in enumerate(top_bot):
        send(cp.at[x2, 0, rows], xr0.at[rows], CX_ID + h, xright)
        send(cp.at[x2, 1, rows], xl0.at[rows], CX_ID + 2 + h, xleft)
    to_other(xm, 2)
    from_core(xp, 1)
    to_other(x, 3)
    from_core(xm, 2)
    for h, rows in enumerate(top_bot):
        arrived(xr0.at[rows], CX_ID + h)
        cpart[core, xp, 0, rows] = cpart[core, xp, 0, rows] + xr0[rows]
        send(cp.at[xp, :, rows], xr1.at[:, rows], CX_ID + 4 + h, xright)
        arrived(xl0.at[rows], CX_ID + 2 + h)
        cpart[core, xm, 1, rows] = cpart[core, xm, 1, rows] + xl0[rows]
        send(cp.at[xm, :, rows], xl1.at[:, rows], CX_ID + 6 + h, xleft)
    from_core(x, 3)
    for i in range(8):
        for h in range(2):
            v = q[0, pl.ds(h * 8 + i, 32, stride=16), :]
            prod_ref[i, 0, pl.ds(h * 32, 32), :] = v[:, :64]
            prod_ref[i, 1, pl.ds(h * 32, 32), :] = v[:, 64:]
    put = pltpu.make_async_copy(prod_ref, prod_hbm, lsem.at[3])
    put.start()
    for h, rows in enumerate(top_bot):
        arrived(xr1.at[:, rows], CX_ID + 4 + h)
        arrived(xl1.at[:, rows], CX_ID + 6 + h)
        cpart[core, x, 1 - yh, rows] = cpart[core, x, 1 - yh, rows] + xr1[1 - yh, rows] + xl1[1 - yh, rows]
        send(cp.at[x, 1 - yh, rows], yrecv.at[rows], CY_ID + h, yfar)
    for h, rows in enumerate(top_bot):
        total = cpart[core, x, yh, rows] + xr1[yh, rows] + xl1[yh, rows]
        arrived(yrecv.at[rows], CY_ID + h)
        total = total + yrecv[rows]
        for b in range(2):
            coarse_ref[h, b] = total[:, b * 64 : b * 64 + 64]

    u = panel.at[0, 0]
    zu = pror.at[0, 0]
    for p in range(2):
        part = u.at[PART[p]]

        @pl.when(jnp.logical_not(own_across))
        def _():
            sent(part, T_ID + p)

        sent(part, Y_ID + p)
        for k in (X_ID, X_ID + 6):
            sent(part, k + p)
            sent(part, k + 2 + p)
            sent(part, k + 4 + p)
    put.wait()
    sent(meta, M_ID)
    for n in range(4):
        sent(alist.at[pl.ds(0, 8)], A_ID + n)
    for n in range(8):
        sent(u, CORE_ID + n)
        sent(zu, PY_ID + n)
    for n in range(3):
        sent(zu, Z_ID + n)
        sent(zu, Z_ID + 4 + n)
    sent(zu.at[PART[0]], Z_ID + 3)
    sent(zu.at[PART[1]], Z_ID + 7)
    piece = q.at[0, pl.ds(0, 256)]
    sent(piece, rs_id(0, 0, 0))
    sent(piece, rs_id(0, 1, 1))
    for step in (1, 2, 3):
        for half in (0, 1):
            for way in (0, 1):
                sent(piece, rs_id(step, half, way))
    for n in range(4):
        sent(crecv.at[0], CC_ID + n)
    for h, rows in enumerate(top_bot):
        sent(xr0.at[rows], CX_ID + h)
        sent(xl0.at[rows], CX_ID + 2 + h)
        sent(xr1.at[:, rows], CX_ID + 4 + h)
        sent(xl1.at[:, rows], CX_ID + 6 + h)
        sent(yrecv.at[rows], CY_ID + h)


def shards(op_tiles, op_rows, op_cols, op_count, pro_tiles, pro_cols, pro_live):
    vmem = pl.BlockSpec(memory_space=pltpu.VMEM)
    smem = pl.BlockSpec(memory_space=pltpu.SMEM)
    anywhere = pl.BlockSpec(memory_space=pl.ANY)
    return pl.pallas_call(
        kernel,
        out_shape=(
            jax.ShapeDtypeStruct((8, 2, 64, 64), F32),
            jax.ShapeDtypeStruct((2, 2, 64, 64), F32),
        ),
        in_specs=[anywhere, vmem, vmem, smem, vmem, smem, smem],
        out_specs=(anywhere, vmem),
        scratch_shapes=[
            pltpu.VMEM((LA, 64, 64), F32),
            pltpu.VMEM((8, 2, 64, 64), F32),
            pltpu.VMEM((8, 128), F32),
            pltpu.VMEM((8, 128), F32),
            pltpu.VMEM((UR, 128), F32),
            pltpu.VMEM((32, LA, 128), F32),
            pltpu.VMEM((32, LA, 128), F32),
            pltpu.VMEM((2, 8, UR, 128), F32),
            pltpu.VMEM((2, 8, UR, 128), F32),
            pltpu.VMEM((2, 512, 512), BF16),
            pltpu.VMEM((2, 512, 512), BF16),
            pltpu.VMEM((2, 512, 256), BF16),
            pltpu.VMEM((2, 512, 256), BF16),
            pltpu.VMEM((8, 512, 128), F32),
            pltpu.VMEM((4, 512, 128), F32),
            pltpu.VMEM((4, 512, 128), F32),
            pltpu.VMEM((2, 4, 256, 512), BF16),
            pltpu.VMEM((2, 4, 256, 512), BF16),
            pltpu.VMEM((512, 256), BF16),
            pltpu.VMEM((2, 4, 2, 128, 128), F32),
            pltpu.VMEM((4, 2, 128, 128), F32),
            pltpu.VMEM((128, 128), F32),
            pltpu.VMEM((128, 128), F32),
            pltpu.VMEM((2, 128, 128), F32),
            pltpu.VMEM((2, 128, 128), F32),
            pltpu.VMEM((128, 128), F32),
            pltpu.SemaphoreType.DMA((N_ID,)),
            pltpu.SemaphoreType.DMA((N_ID,)),
            pltpu.SemaphoreType.DMA((4,)),
        ],
        compiler_params=pltpu.CompilerParams(
            collective_id=0, has_side_effects=True, vmem_limit_bytes=60 * 1024 * 1024
        ),
    )(
        op_tiles.reshape(32, 64, 64), op_rows.T, op_cols.T, op_count,
        pro_tiles.reshape(8, 64, 64), pro_cols.T, pro_live.T,
    )


def solution(mesh):
    return jax.shard_map(
        shards,
        mesh=mesh,
        in_specs=(
            P("row", "col", None, None),
            P("row", "col"),
            P("row", "col"),
            P("row", "col"),
            P("row", "col", None, None),
            P("row", "col"),
            P("row", "col"),
        ),
        out_specs=(P("row", "col", None, None), P("row", "col", None, None)),
        check_vma=False,
    )
```

```python
import functools

import jax
import jax.numpy as jnp
from jax import lax
from jax.experimental import pallas as pl
from jax.experimental.pallas import tpu as pltpu
from jax.sharding import PartitionSpec as P

MESH = pl.DeviceIdType.MESH
F32, BF16 = jnp.float32, jnp.bfloat16
UR = 264
UH = 136
LA = 32
ORDER = ((1, 0, 3, 2), (0, 1, 2, 3))
PART = (pl.ds(0, UH), pl.ds(UH, UR - UH))

M_ID = 0
A_ID = 1
T_ID = 5
Y_ID = 7
X_ID = 9
CORE_ID = 21
Z_ID = 29
PY_ID = 37
RS_ID = 45
CC_ID = 77
CX_ID = 85
CY_ID = 93
H_ID = 95
F_ID = 96
N_ID = 97


def split(v):
    hi = v.astype(BF16)
    return hi, (v - hi.astype(F32)).astype(BF16)


def pack(tile):
    return jnp.concatenate([tile[:32], tile[32:]], axis=1)


def kernel(
    op_hbm, rows_ref, cols_ref, count_ref, pro_ref, pcols_ref, plive_ref,
    prod_hbm, coarse_ref,
    op_ref, prod_ref, meta, mnear, hop,
    unit, alist, anear, panel, pror, ahi, alo, rhi, rlo, q, rsr, rsl, pthi, ptlo, pcat,
    cpart, crecv, xr0, xl0, xr1, xl1, yrecv,
    ssem, rsem, lsem,
):
    r = lax.axis_index("row")
    c = lax.axis_index("col")
    yh, x, core = r // 8, lax.rem(r // 2, 4), lax.rem(r, 2)
    yl, z = c // 8, lax.rem(c, 8)

    def rowdev(yh_, x_, core_):
        return ((yh_ * 4 + x_) * 2 + core_, c)

    ynear = (r, (1 - yl) * 8 + z)
    zright, zleft = (r, yl * 8 + lax.rem(z + 1, 8)), (r, yl * 8 + lax.rem(z + 7, 8))
    xright, xleft = rowdev(yh, lax.rem(x + 1, 4), core), rowdev(yh, lax.rem(x + 3, 4), core)
    yfar = rowdev(1 - yh, x, core)
    other = rowdev(yh, x, 1 - core)
    turn = 8 - z // 2 - 2 * lax.rem(z, 2)
    s0 = 4 * core + lax.rem(x + turn, 4)
    plane = 2 * x + core
    across = rowdev(yh, lax.rem(z + x + 2 * core, 4), z // 4)[0], yl * 8 + plane
    source = rowdev(yh, z // 2, lax.rem(z, 2))[0], yl * 8 + s0
    own_across = jnp.logical_and(s0 == z, plane == z)
    via_x, via_src_x = lax.rem(z + x + 2 * core, 4), lax.rem(x + 12 - z - 2 * core, 4)
    via, via_src = rowdev(yh, via_x, core), rowdev(yh, via_src_x, core)
    via_self = via_x == x
    via_last = jnp.logical_and(plane == z, z // 4 == core)
    fwd_plane = 2 * via_src_x + core
    fwd = rowdev(yh, x, z // 4)[0], yl * 8 + fwd_plane
    fwd_src = rowdev(yh, x, lax.rem(z, 2))[0], yl * 8 + s0
    fwd_self = jnp.logical_and(fwd_plane == z, z // 4 == core)
    direct = jnp.logical_and(via_self, jnp.logical_not(own_across))
    final_hop = jnp.logical_and(jnp.logical_not(via_self), via_last)
    first_hop = jnp.logical_not(jnp.logical_or(via_self, via_last))
    serves = jnp.logical_not(jnp.logical_or(via_self, fwd_self))

    def send(src, dst, k, dev):
        pltpu.make_async_remote_copy(
            src_ref=src, dst_ref=dst, send_sem=ssem.at[k], recv_sem=rsem.at[k], device_id=dev, device_id_type=MESH
        ).start()

    def arrived(dst, k):
        pltpu.make_async_remote_copy(
            src_ref=dst, dst_ref=dst, send_sem=ssem.at[k], recv_sem=rsem.at[k], device_id=ynear, device_id_type=MESH
        ).wait_recv()

    def sent(src, k):
        pltpu.make_async_remote_copy(
            src_ref=src, dst_ref=src, send_sem=ssem.at[k], recv_sem=rsem.at[k], device_id=ynear, device_id_type=MESH
        ).wait_send()

    fetch = pltpu.make_async_copy(op_hbm, op_ref, lsem.at[2])
    fetch.start()
    barrier = pltpu.get_barrier_semaphore()
    for dev in (ynear, zright, zleft, xright, xleft, yfar, other):
        pl.semaphore_signal(barrier, inc=1, device_id=dev, device_id_type=MESH)

    @pl.when(jnp.logical_not(own_across))
    def _():
        pl.semaphore_signal(barrier, inc=1, device_id=across, device_id_type=MESH)
        pl.semaphore_signal(barrier, inc=1, device_id=source, device_id_type=MESH)

    @pl.when(jnp.logical_not(via_self))
    def _():
        pl.semaphore_signal(barrier, inc=1, device_id=via, device_id_type=MESH)
        pl.semaphore_signal(barrier, inc=1, device_id=via_src, device_id_type=MESH)

    @pl.when(jnp.logical_not(fwd_self))
    def _():
        pl.semaphore_signal(barrier, inc=1, device_id=fwd, device_id_type=MESH)
        pl.semaphore_signal(barrier, inc=1, device_id=fwd_src, device_id_type=MESH)

    for k in range(8):
        live = plive_ref[0, k].astype(F32)
        unit[pl.ds(k * 32, 32), :] = pack(pro_ref[k]) * live
        unit[pl.ds(256 + k, 1), :] = jnp.full((1, 128), pcols_ref[0, k].astype(F32))

    pl.semaphore_wait(
        barrier,
        7 + jnp.where(own_across, 0, 2) + jnp.where(via_self, 0, 2) + jnp.where(fwd_self, 0, 2),
    )

    @pl.when(own_across)
    def _():
        pltpu.make_async_copy(unit, panel.at[yh, z], lsem.at[0]).start()

    @pl.when(jnp.logical_not(own_across))
    def _():
        send(unit.at[PART[0]], panel.at[yh, z].at[PART[0]], T_ID, across)

    @pl.when(direct)
    def _():
        send(unit.at[PART[1]], panel.at[yh, z].at[PART[1]], T_ID + 1, across)

    @pl.when(final_hop)
    def _():
        send(unit.at[PART[1]], panel.at[yh, z].at[PART[1]], T_ID + 1, via)

    @pl.when(first_hop)
    def _():
        send(unit.at[PART[1]], hop, H_ID, via)

    keep = pltpu.make_async_copy(unit, pror.at[yl, z], lsem.at[1])
    keep.start()

    pos = rows_ref[...] * 8 + cols_ref[...]
    live_slot = lax.broadcasted_iota(jnp.int32, (1, LA), 1) < count_ref[0, 0]
    pos = jnp.where(live_slot, pos, -1).astype(F32)
    meta[...] = jnp.zeros((8, 128), F32)
    meta[pl.ds(0, 1), pl.ds(0, LA)] = pos
    meta[pl.ds(0, 1), pl.ds(LA, LA)] = pos
    send(meta, mnear, M_ID, ynear)
    fetch.wait()

    def pack_piece(n):
        def slot(t, carry):
            a = op_ref[t, pl.ds(n * 8, 8), :]
            b = op_ref[t, pl.ds(32 + n * 8, 8), :]
            alist[pl.ds(n * 8, 8), t, :] = jnp.concatenate([a, b], axis=1)
            return carry

        lax.fori_loop(0, LA, slot, 0, unroll=8)

    def send_piece(n):
        at = pl.ds(n * 8, 8)
        send(alist.at[at], anear.at[at], A_ID + n, ynear)

    for n in range(4):
        pack_piece(n)
        if n < 2:
            send_piece(n)

    left32 = lax.broadcasted_iota(jnp.int32, (32, 128), 1) < 64
    left8 = lax.broadcasted_iota(jnp.int32, (8, 128), 1) < 64
    place = lax.broadcasted_iota(jnp.int32, (64, 2 * LA), 0)
    place = (lax.rem(place, 8) * 8 + place // 8).astype(F32)

    def dot(a, b):
        return lax.dot_general(a, b, (((1,), (0,)), ((), ())), preferred_element_type=F32)

    def build_a(src, which, at, n):
        hot = (which[pl.ds(0, 1), pl.ds(0, 2 * LA)] == place).astype(F32).astype(BF16)

        def row(step, carry):
            rho = n * 8 + step * 4
            columns = []
            for e in range(4):
                columns.append(jnp.concatenate(split(src[rho + e]), axis=0))
            tiles = dot(hot, jnp.concatenate(columns, axis=1))
            for e in range(4):
                t = tiles[:, e * 128 : e * 128 + 128]
                for m in range(4):
                    even, odd = t[m * 16 : m * 16 + 8], t[m * 16 + 8 : m * 16 + 16]
                    top = jnp.where(left8, even, pltpu.roll(odd, 64, 1))
                    bot = jnp.where(left8, pltpu.roll(even, 64, 1), odd)
                    hi, lo = split(jnp.concatenate([top, bot], axis=0))
                    at_rows = pl.ds(pl.multiple_of((rho + e) * 16, 16), 16)
                    ahi[at, at_rows, pl.ds(m * 128, 128)] = hi
                    alo[at, at_rows, pl.ds(m * 128, 128)] = lo
            return carry

        lax.fori_loop(0, 2, row, 0, unroll=2)

    def dense(ref, b, s, k):
        tile = ref[b, s, pl.ds(k * 32, 32), :]
        col = ref[b, s, pl.ds(256 + k, 1), :]
        turned = pltpu.roll(tile, 64, 1)
        a, bb = 1.0 - col, col
        top = jnp.where(left32, tile * a, turned * bb)
        bot = jnp.where(left32, turned * a, tile * bb)
        return top, bot

    zu = pror.at[yl, z]
    build_a(alist, meta, yl, 0)

    @pl.when(serves)
    def _():
        arrived(hop, H_ID)
        pltpu.make_async_remote_copy(
            src_ref=hop,
            dst_ref=panel.at[yh, z].at[PART[1]],
            send_sem=ssem.at[F_ID],
            recv_sem=rsem.at[T_ID + 1],
            device_id=fwd,
            device_id_type=MESH,
        ).start()

    def ring(off):
        return 4 * core + lax.rem(x + turn + off, 4)

    mine, theirs = yh, 1 - yh
    sl, sr, sf = ring(3), ring(1), ring(2)

    def spread(b, k, p):
        u = panel.at[b, s0].at[PART[p]]
        send(u, u, k + p, xright)
        send(u, u, k + 2 + p, xleft)

    def onward(b, k):
        u = panel.at[b, sl].at[PART[0]]
        arrived(u, k)
        send(u, u, k + 4, xright)
        u = panel.at[b, sr].at[PART[1]]
        arrived(u, k + 3)
        send(u, u, k + 5, xleft)

    def beside(b, k, kc):
        u = panel.at[b, sl]
        arrived(u.at[PART[1]], k + 1)
        send(u, u, kc + 1, other)
        u = panel.at[b, sr]
        arrived(u.at[PART[0]], k + 2)
        send(u, u, kc + 2, other)

    def far(b, k, kc):
        u = panel.at[b, sf]
        arrived(u.at[PART[0]], k + 4)
        arrived(u.at[PART[1]], k + 5)
        send(u, u, kc + 3, other)

    def zstep(step):
        got_r = pror.at[yl, lax.rem(z + 8 - step, 8)]
        got_l = pror.at[yl, lax.rem(z + step, 8)]
        arrived(got_r, Z_ID + step - 1)
        arrived(got_l, Z_ID + 4 + step - 1)
        if step < 3:
            send(got_r, got_r, Z_ID + step, zright)
            send(got_l, got_l, Z_ID + 4 + step, zleft)
        else:
            send(got_r.at[PART[0]], got_r.at[PART[0]], Z_ID + 3, zright)
            send(got_l.at[PART[1]], got_l.at[PART[1]], Z_ID + 7, zleft)
        send(got_r, got_r, PY_ID + 2 * step - 1, ynear)
        send(got_l, got_l, PY_ID + 2 * step, ynear)

    u = panel.at[mine, s0]

    @pl.when(own_across)
    def _():
        pltpu.make_async_copy(unit, panel.at[yh, z], lsem.at[0]).wait()

    for p in range(2):
        @pl.when(jnp.logical_not(own_across))
        def _():
            arrived(u.at[PART[p]], T_ID + p)

        send(u.at[PART[p]], u.at[PART[p]], Y_ID + p, yfar)
        spread(mine, X_ID, p)
    send_piece(2)
    send_piece(3)
    send(u, u, CORE_ID, other)
    keep.wait()
    send(unit, zu, Z_ID, zright)
    send(unit, zu, Z_ID + 4, zleft)
    send(zu, zu, PY_ID, ynear)
    build_a(alist, meta, yl, 1)
    onward(mine, X_ID)
    build_a(alist, meta, yl, 2)
    u = panel.at[theirs, s0]
    for p in range(2):
        arrived(u.at[PART[p]], Y_ID + p)
        spread(theirs, X_ID + 6, p)
    send(u, u, CORE_ID + 4, other)
    zstep(1)
    beside(mine, X_ID, CORE_ID)
    build_a(alist, meta, yl, 3)
    onward(theirs, X_ID + 6)
    far(mine, X_ID, CORE_ID)
    zstep(2)
    arrived(mnear, M_ID)
    for n in range(2):
        arrived(anear.at[pl.ds(n * 8, 8)], A_ID + n)
        build_a(anear, mnear, 1 - yl, n)
    beside(theirs, X_ID + 6, CORE_ID + 4)
    far(theirs, X_ID + 6, CORE_ID + 4)
    for n in range(2, 4):
        arrived(anear.at[pl.ds(n * 8, 8)], A_ID + n)
        build_a(anear, mnear, 1 - yl, n)
    for n in range(8):
        s = 4 * (1 - core) + lax.rem(x + turn + (0, 3, 1, 2)[n % 4], 4)
        arrived(panel.at[(mine, theirs)[n // 4], s], CORE_ID + n)

    def build_r(d, at):
        s = lax.rem(z + d, 8)

        def block(b, carry):
            for k in range(8):
                for off, v in zip((0, 32), dense(panel, b, s, k)):
                    hi, lo = split(v)
                    rhi[b, pl.ds(k * 64 + off, 32), pl.ds(at * 128, 128)] = hi
                    rlo[b, pl.ds(k * 64 + off, 32), pl.ds(at * 128, 128)] = lo
            return carry

        lax.fori_loop(0, 2, block, 0)

    left128 = lax.broadcasted_iota(jnp.int32, (128, 128), 1) < 64
    left64 = lax.broadcasted_iota(jnp.int32, (64, 128), 1) < 64

    def chunk(*ds):
        wide = 128 * len(ds)
        for at, d in enumerate(ds):
            build_r(d, at)

        def part(e, carry):
            acc = jnp.zeros((256, wide), F32)
            top = pl.ds(pl.multiple_of(e * 128, 128), 128)
            bot = pl.ds(pl.multiple_of(256 + e * 128, 128), 128)
            for b in range(2):
                h = jnp.concatenate([ahi[b, top, :], ahi[b, bot, :]], axis=0)
                l = jnp.concatenate([alo[b, top, :], alo[b, bot, :]], axis=0)
                rh = rhi[b, :, pl.ds(0, wide)]
                acc = acc + dot(h, rh) + dot(h, rlo[b, :, pl.ds(0, wide)]) + dot(l, rh)
            for at, d in enumerate(ds):
                t, u = acc[:128, at * 128 : at * 128 + 128], acc[128:, at * 128 : at * 128 + 128]
                q[d, e] = jnp.where(left128, t, pltpu.roll(u, 64, 1))
                q[d, 2 + e] = jnp.where(left128, pltpu.roll(t, 64, 1), u)
            return carry

        lax.fori_loop(0, 2, part, 0)

    def rs_id(step, blk, way):
        return RS_ID + (step * 4 + blk) * 2 + way

    def rs_send(d, step, blk, way):
        buf = (rsr, rsl)[way]
        send(q.at[d, blk], buf.at[step, blk], rs_id(step, blk, way), (zright, zleft)[way])

    def rs_add(d, step, blk, way):
        buf = (rsr, rsl)[way]
        arrived(buf.at[step, blk], rs_id(step, blk, way))
        q[d, blk] = q[d, blk] + buf[step, blk]

    def build_t(b, s):
        flag = pror[b, s, pl.ds(256, 8), :]
        for m in range(4):
            parts = []
            for rho in range(8 * m, 8 * m + 8):
                tile = pror[b, s, pl.ds(rho, 8, stride=32), :]
                turned = pltpu.roll(tile, 64, 1)
                parts.append(jnp.where(left8, tile * (1.0 - flag), turned * flag))
                parts.append(jnp.where(left8, turned * (1.0 - flag), tile * flag))
            hi, lo = split(jnp.concatenate(parts, axis=0).T)
            g = b * 8 + s
            rows = pl.ds(pl.multiple_of(g // 8 * 128, 128), 128)
            pthi[lax.rem(g, 2), lax.rem(g // 2, 4), rows, pl.ds(m * 128, 128)] = hi
            ptlo[lax.rem(g, 2), lax.rem(g // 2, 4), rows, pl.ds(m * 128, 128)] = lo

    def own_t(s, carry):
        build_t(yl, s)
        return carry

    def pass_step(step):
        for n in range(4):
            for way, d in ((0, 4 - step), (1, 4 + step)):
                blk = ORDER[way][n]
                if step > 1 or blk % 2 == way:
                    rs_add(d, step - 1, blk, way)
                rs_send(d, step, blk, way)

    zstep(3)
    chunk(4)
    for blk in range(4):
        rs_send(4, 0, blk, blk % 2)
    chunk(3, 5)
    pass_step(1)
    zfar = pror.at[yl, lax.rem(z + 4, 8)]
    arrived(zfar.at[PART[0]], Z_ID + 3)
    arrived(zfar.at[PART[1]], Z_ID + 7)
    send(zfar, zfar, PY_ID + 7, ynear)
    chunk(2, 6)
    lax.fori_loop(0, 8, own_t, 0)
    pass_step(2)
    chunk(1, 7)
    chunk(0)
    pass_step(3)

    near = [z]
    for step in (1, 2, 3):
        near += [lax.rem(z + 8 - step, 8), lax.rem(z + step, 8)]
    near.append(lax.rem(z + 4, 8))
    for n, shard in enumerate(near):
        arrived(pror.at[1 - yl, shard], PY_ID + n)
        build_t(1 - yl, shard)

    def finish(m):
        for e in range(2):
            for way in (0, 1):
                rs_add(0, 3, 2 * m + e, way)
            v = q[0, 2 * m + e]
            hi = v.astype(BF16).astype(F32)
            lo = v - hi
            pcat[m, pl.ds(e * 128, 128), :] = jnp.where(left128, hi, pltpu.roll(lo, 64, 1)).astype(BF16)
            pcat[m, pl.ds(256 + e * 128, 128), :] = jnp.where(left128, pltpu.roll(hi, 64, 1), lo).astype(BF16)

    def coarse_part(gc, gx, m):
        a = dot(pthi[gc, gx], pcat[m])
        v = a + pltpu.roll(a, 64, 1) + dot(ptlo[gc, gx], pcat[m])
        for gy in range(2):
            top, bot = v[gy * 128 : gy * 128 + 64], v[gy * 128 + 64 : gy * 128 + 128]
            cpart[gc, gx, m, gy] = jnp.where(left64, top, pltpu.roll(bot, 64, 1))

    def to_other(gx, m, n):
        coarse_part(1 - core, gx, m)
        send(cpart.at[1 - core, gx, m], crecv.at[gx, m], CC_ID + 4 * m + n, other)

    def from_core(gx, m, n):
        coarse_part(core, gx, m)
        arrived(crecv.at[gx, m], CC_ID + 4 * m + n)
        cpart[core, gx, m] = cpart[core, gx, m] + crecv[gx, m]

    x2 = lax.rem(x + 2, 4)
    xp, xm = lax.rem(x + 1, 4), lax.rem(x + 3, 4)
    cp = cpart.at[core]

    def first(m):
        to_other(x2, m, 0)
        to_other(xp, m, 1)
        from_core(x2, m, 0)
        send(cp.at[x2, m, 0], xr0.at[m], CX_ID + 4 * m, xright)
        send(cp.at[x2, m, 1], xl0.at[m], CX_ID + 4 * m + 1, xleft)

    def sides(m):
        to_other(xm, m, 2)
        from_core(xp, m, 1)
        from_core(xm, m, 2)

    def second(m):
        arrived(xr0.at[m], CX_ID + 4 * m)
        cpart[core, xp, m, 0] = cpart[core, xp, m, 0] + xr0[m]
        send(cp.at[xp, m], xr1.at[m], CX_ID + 4 * m + 2, xright)
        arrived(xl0.at[m], CX_ID + 4 * m + 1)
        cpart[core, xm, m, 1] = cpart[core, xm, m, 1] + xl0[m]
        send(cp.at[xm, m], xl1.at[m], CX_ID + 4 * m + 3, xleft)

    def third(m):
        arrived(xr1.at[m], CX_ID + 4 * m + 2)
        arrived(xl1.at[m], CX_ID + 4 * m + 3)
        cpart[core, x, m, 1 - yh] = cpart[core, x, m, 1 - yh] + xr1[m, 1 - yh] + xl1[m, 1 - yh]
        send(cp.at[x, m, 1 - yh], yrecv.at[m], CY_ID + m, yfar)

    finish(0)
    first(0)
    finish(1)
    first(1)
    sides(0)
    second(0)
    sides(1)
    second(1)
    to_other(x, 0, 3)
    to_other(x, 1, 3)
    from_core(x, 0, 3)
    third(0)
    from_core(x, 1, 3)
    for i in range(8):
        for h in range(2):
            for m in range(2):
                for e in range(2):
                    v = q[0, 2 * m + e, pl.ds(h * 8 + i, 8, stride=16), :]
                    prod_ref[i, m, pl.ds(h * 32 + e * 8, 8), :] = v[:, :64]
                    prod_ref[i, m, pl.ds(h * 32 + 16 + e * 8, 8), :] = v[:, 64:]
    put = pltpu.make_async_copy(prod_ref, prod_hbm, lsem.at[3])
    put.start()
    third(1)
    for m in range(2):
        total = cpart[core, x, m, yh] + xr1[m, yh] + xl1[m, yh]
        arrived(yrecv.at[m], CY_ID + m)
        total = total + yrecv[m]
        coarse_ref[0, m] = total[:, :64]
        coarse_ref[1, m] = total[:, 64:]

    u = panel.at[0, 0]

    @pl.when(jnp.logical_not(own_across))
    def _():
        sent(u.at[PART[0]], T_ID)

    @pl.when(jnp.logical_or(direct, final_hop))
    def _():
        sent(u.at[PART[1]], T_ID + 1)

    @pl.when(first_hop)
    def _():
        sent(hop, H_ID)

    @pl.when(serves)
    def _():
        sent(hop, F_ID)

    zu = pror.at[0, 0]
    for p in range(2):
        part = u.at[PART[p]]

        sent(part, Y_ID + p)
        for k in (X_ID, X_ID + 6):
            sent(part, k + p)
            sent(part, k + 2 + p)
            sent(part, k + 4 + p)
    put.wait()
    sent(meta, M_ID)
    for n in range(4):
        sent(alist.at[pl.ds(0, 8)], A_ID + n)
    for n in range(8):
        sent(u, CORE_ID + n)
        sent(zu, PY_ID + n)
    for n in range(3):
        sent(zu, Z_ID + n)
        sent(zu, Z_ID + 4 + n)
    sent(zu.at[PART[0]], Z_ID + 3)
    sent(zu.at[PART[1]], Z_ID + 7)
    piece = q.at[0, 0]
    for blk in range(4):
        sent(piece, rs_id(0, blk, blk % 2))
        for step in (1, 2, 3):
            for way in (0, 1):
                sent(piece, rs_id(step, blk, way))
    for n in range(8):
        sent(crecv.at[0, 0], CC_ID + n)
    for m in range(2):
        sent(xr0.at[m], CX_ID + 4 * m)
        sent(xl0.at[m], CX_ID + 4 * m + 1)
        sent(xr1.at[m], CX_ID + 4 * m + 2)
        sent(xl1.at[m], CX_ID + 4 * m + 3)
        sent(yrecv.at[m], CY_ID + m)


def shards(op_tiles, op_rows, op_cols, op_count, pro_tiles, pro_cols, pro_live):
    vmem = pl.BlockSpec(memory_space=pltpu.VMEM)
    smem = pl.BlockSpec(memory_space=pltpu.SMEM)
    anywhere = pl.BlockSpec(memory_space=pl.ANY)
    return pl.pallas_call(
        kernel,
        out_shape=(
            jax.ShapeDtypeStruct((8, 2, 64, 64), F32),
            jax.ShapeDtypeStruct((2, 2, 64, 64), F32),
        ),
        in_specs=[anywhere, vmem, vmem, smem, vmem, smem, smem],
        out_specs=(anywhere, vmem),
        scratch_shapes=[
            pltpu.VMEM((LA, 64, 64), F32),
            pltpu.VMEM((8, 2, 64, 64), F32),
            pltpu.VMEM((8, 128), F32),
            pltpu.VMEM((8, 128), F32),
            pltpu.VMEM((UR - UH, 128), F32),
            pltpu.VMEM((UR, 128), F32),
            pltpu.VMEM((32, LA, 128), F32),
            pltpu.VMEM((32, LA, 128), F32),
            pltpu.VMEM((2, 8, UR, 128), F32),
            pltpu.VMEM((2, 8, UR, 128), F32),
            pltpu.VMEM((2, 512, 512), BF16),
            pltpu.VMEM((2, 512, 512), BF16),
            pltpu.VMEM((2, 512, 256), BF16),
            pltpu.VMEM((2, 512, 256), BF16),
            pltpu.VMEM((8, 4, 128, 128), F32),
            pltpu.VMEM((4, 4, 128, 128), F32),
            pltpu.VMEM((4, 4, 128, 128), F32),
            pltpu.VMEM((2, 4, 256, 512), BF16),
            pltpu.VMEM((2, 4, 256, 512), BF16),
            pltpu.VMEM((2, 512, 128), BF16),
            pltpu.VMEM((2, 4, 2, 2, 64, 128), F32),
            pltpu.VMEM((4, 2, 2, 64, 128), F32),
            pltpu.VMEM((2, 64, 128), F32),
            pltpu.VMEM((2, 64, 128), F32),
            pltpu.VMEM((2, 2, 64, 128), F32),
            pltpu.VMEM((2, 2, 64, 128), F32),
            pltpu.VMEM((2, 64, 128), F32),
            pltpu.SemaphoreType.DMA((N_ID,)),
            pltpu.SemaphoreType.DMA((N_ID,)),
            pltpu.SemaphoreType.DMA((4,)),
        ],
        compiler_params=pltpu.CompilerParams(
            collective_id=0, has_side_effects=True, vmem_limit_bytes=60 * 1024 * 1024
        ),
    )(
        op_tiles.reshape(32, 64, 64), op_rows.T, op_cols.T, op_count,
        pro_tiles.reshape(8, 64, 64), pro_cols.T, pro_live.T,
    )


def solution(mesh):
    return jax.shard_map(
        shards,
        mesh=mesh,
        in_specs=(
            P("row", "col", None, None),
            P("row", "col"),
            P("row", "col"),
            P("row", "col"),
            P("row", "col", None, None),
            P("row", "col"),
            P("row", "col"),
        ),
        out_specs=(P("row", "col", None, None), P("row", "col", None, None)),
        check_vma=False,
    )
```

```python
import functools

import jax
import jax.numpy as jnp
from jax import lax
from jax.experimental import pallas as pl
from jax.experimental.pallas import tpu as pltpu
from jax.sharding import PartitionSpec as P

MESH = pl.DeviceIdType.MESH
F32, BF16 = jnp.float32, jnp.bfloat16
UR = 264
UH = 136
LA = 32
ORDER = ((1, 0, 3, 2), (0, 1, 2, 3))
PART = (pl.ds(0, UH), pl.ds(UH, UR - UH))

M_ID = 0
A_ID = 1
T_ID = 5
Y_ID = 7
X_ID = 9
CORE_ID = 21
Z_ID = 29
PY_ID = 37
RS_ID = 45
CC_ID = 77
CX_ID = 85
CY_ID = 93
H_ID = 95
F_ID = 96
N_ID = 97


def split(v):
    hi = v.astype(BF16)
    return hi, (v - hi.astype(F32)).astype(BF16)


def pack(tile):
    return jnp.concatenate([tile[:32], tile[32:]], axis=1)


def kernel(
    op_hbm, rows_ref, cols_ref, count_ref, pro_ref, pcols_ref, plive_ref,
    prod_hbm, coarse_ref,
    op_ref, prod_ref, meta, mnear, hop,
    unit, alist, anear, panel, pror, ahi, alo, rhi, rlo, q, rsr, rsl, pthi, ptlo, pcat,
    cpart, crecv, xr0, xl0, xr1, xl1, yrecv,
    ssem, rsem, lsem,
):
    r = lax.axis_index("row")
    c = lax.axis_index("col")
    yh, x, core = r // 8, lax.rem(r // 2, 4), lax.rem(r, 2)
    yl, z = c // 8, lax.rem(c, 8)

    def rowdev(yh_, x_, core_):
        return ((yh_ * 4 + x_) * 2 + core_, c)

    ynear = (r, (1 - yl) * 8 + z)
    zright, zleft = (r, yl * 8 + lax.rem(z + 1, 8)), (r, yl * 8 + lax.rem(z + 7, 8))
    xright, xleft = rowdev(yh, lax.rem(x + 1, 4), core), rowdev(yh, lax.rem(x + 3, 4), core)
    yfar = rowdev(1 - yh, x, core)
    other = rowdev(yh, x, 1 - core)
    turn = 8 - z // 2 - 2 * lax.rem(z, 2)
    s0 = 4 * core + lax.rem(x + turn, 4)
    plane = 2 * x + core
    across = rowdev(yh, lax.rem(z + x + 2 * core, 4), z // 4)[0], yl * 8 + plane
    source = rowdev(yh, z // 2, lax.rem(z, 2))[0], yl * 8 + s0
    own_across = jnp.logical_and(s0 == z, plane == z)
    via_x, via_src_x = lax.rem(z + x + 2 * core, 4), lax.rem(x + 12 - z - 2 * core, 4)
    via, via_src = rowdev(yh, via_x, core), rowdev(yh, via_src_x, core)
    via_self = via_x == x
    via_last = jnp.logical_and(plane == z, z // 4 == core)
    fwd_plane = 2 * via_src_x + core
    fwd = rowdev(yh, x, z // 4)[0], yl * 8 + fwd_plane
    fwd_src = rowdev(yh, x, lax.rem(z, 2))[0], yl * 8 + s0
    fwd_self = jnp.logical_and(fwd_plane == z, z // 4 == core)
    direct = jnp.logical_and(via_self, jnp.logical_not(own_across))
    final_hop = jnp.logical_and(jnp.logical_not(via_self), via_last)
    first_hop = jnp.logical_not(jnp.logical_or(via_self, via_last))
    serves = jnp.logical_not(jnp.logical_or(via_self, fwd_self))

    def send(src, dst, k, dev):
        pltpu.make_async_remote_copy(
            src_ref=src, dst_ref=dst, send_sem=ssem.at[k], recv_sem=rsem.at[k], device_id=dev, device_id_type=MESH
        ).start()

    def arrived(dst, k):
        pltpu.make_async_remote_copy(
            src_ref=dst, dst_ref=dst, send_sem=ssem.at[k], recv_sem=rsem.at[k], device_id=ynear, device_id_type=MESH
        ).wait_recv()

    def sent(src, k):
        pltpu.make_async_remote_copy(
            src_ref=src, dst_ref=src, send_sem=ssem.at[k], recv_sem=rsem.at[k], device_id=ynear, device_id_type=MESH
        ).wait_send()

    fetch = pltpu.make_async_copy(op_hbm, op_ref, lsem.at[2])
    fetch.start()
    barrier = pltpu.get_barrier_semaphore()
    for dev in (ynear, zright, zleft, xright, xleft, yfar, other):
        pl.semaphore_signal(barrier, inc=1, device_id=dev, device_id_type=MESH)

    @pl.when(jnp.logical_not(own_across))
    def _():
        pl.semaphore_signal(barrier, inc=1, device_id=across, device_id_type=MESH)
        pl.semaphore_signal(barrier, inc=1, device_id=source, device_id_type=MESH)

    @pl.when(jnp.logical_not(via_self))
    def _():
        pl.semaphore_signal(barrier, inc=1, device_id=via, device_id_type=MESH)
        pl.semaphore_signal(barrier, inc=1, device_id=via_src, device_id_type=MESH)

    @pl.when(jnp.logical_not(fwd_self))
    def _():
        pl.semaphore_signal(barrier, inc=1, device_id=fwd, device_id_type=MESH)
        pl.semaphore_signal(barrier, inc=1, device_id=fwd_src, device_id_type=MESH)

    for k in range(8):
        live = plive_ref[0, k].astype(F32)
        unit[pl.ds(k * 32, 32), :] = pack(pro_ref[k]) * live
        unit[pl.ds(256 + k, 1), :] = jnp.full((1, 128), pcols_ref[0, k].astype(F32))

    pl.semaphore_wait(
        barrier,
        7 + jnp.where(own_across, 0, 2) + jnp.where(via_self, 0, 2) + jnp.where(fwd_self, 0, 2),
    )

    @pl.when(own_across)
    def _():
        pltpu.make_async_copy(unit, panel.at[yh, z], lsem.at[0]).start()

    @pl.when(jnp.logical_not(own_across))
    def _():
        send(unit.at[PART[0]], panel.at[yh, z].at[PART[0]], T_ID, across)

    @pl.when(direct)
    def _():
        send(unit.at[PART[1]], panel.at[yh, z].at[PART[1]], T_ID + 1, across)

    @pl.when(final_hop)
    def _():
        send(unit.at[PART[1]], panel.at[yh, z].at[PART[1]], T_ID + 1, via)

    @pl.when(first_hop)
    def _():
        send(unit.at[PART[1]], hop, H_ID, via)

    keep = pltpu.make_async_copy(unit, pror.at[yl, z], lsem.at[1])
    keep.start()

    pos = rows_ref[...] * 8 + cols_ref[...]
    live_slot = lax.broadcasted_iota(jnp.int32, (1, LA), 1) < count_ref[0, 0]
    pos = jnp.where(live_slot, pos, -1).astype(F32)
    meta[...] = jnp.zeros((8, 128), F32)
    meta[pl.ds(0, 1), pl.ds(0, LA)] = pos
    meta[pl.ds(0, 1), pl.ds(LA, LA)] = pos
    send(meta, mnear, M_ID, ynear)
    fetch.wait()

    def pack_piece(n):
        def slot(t, carry):
            a = op_ref[t, pl.ds(n * 8, 8), :]
            b = op_ref[t, pl.ds(32 + n * 8, 8), :]
            alist[pl.ds(n * 8, 8), t, :] = jnp.concatenate([a, b], axis=1)
            return carry

        lax.fori_loop(0, LA, slot, 0, unroll=8)

    def send_piece(n):
        at = pl.ds(n * 8, 8)
        send(alist.at[at], anear.at[at], A_ID + n, ynear)

    for n in range(4):
        pack_piece(n)
        if n < 2:
            send_piece(n)

    left32 = lax.broadcasted_iota(jnp.int32, (32, 128), 1) < 64
    left8 = lax.broadcasted_iota(jnp.int32, (8, 128), 1) < 64
    place = lax.broadcasted_iota(jnp.int32, (64, 2 * LA), 0)
    place = (lax.rem(place, 8) * 8 + place // 8).astype(F32)

    def dot(a, b):
        return lax.dot_general(a, b, (((1,), (0,)), ((), ())), preferred_element_type=F32)

    def build_a(src, which, at, n):
        hot = (which[pl.ds(0, 1), pl.ds(0, 2 * LA)] == place).astype(F32).astype(BF16)

        def row(step, carry):
            rho = n * 8 + step * 4
            columns = []
            for e in range(4):
                columns.append(jnp.concatenate(split(src[rho + e]), axis=0))
            tiles = dot(hot, jnp.concatenate(columns, axis=1))
            for e in range(4):
                t = tiles[:, e * 128 : e * 128 + 128]
                for m in range(4):
                    even, odd = t[m * 16 : m * 16 + 8], t[m * 16 + 8 : m * 16 + 16]
                    top = jnp.where(left8, even, pltpu.roll(odd, 64, 1))
                    bot = jnp.where(left8, pltpu.roll(even, 64, 1), odd)
                    hi, lo = split(jnp.concatenate([top, bot], axis=0))
                    at_rows = pl.ds(pl.multiple_of((rho + e) * 16, 16), 16)
                    ahi[at, at_rows, pl.ds(m * 128, 128)] = hi
                    alo[at, at_rows, pl.ds(m * 128, 128)] = lo
            return carry

        lax.fori_loop(0, 2, row, 0, unroll=2)

    def dense(ref, b, s, k):
        tile = ref[b, s, pl.ds(k * 32, 32), :]
        col = ref[b, s, pl.ds(256 + k, 1), :]
        turned = pltpu.roll(tile, 64, 1)
        a, bb = 1.0 - col, col
        top = jnp.where(left32, tile * a, turned * bb)
        bot = jnp.where(left32, turned * a, tile * bb)
        return top, bot

    zu = pror.at[yl, z]
    build_a(alist, meta, yl, 0)

    @pl.when(serves)
    def _():
        arrived(hop, H_ID)
        pltpu.make_async_remote_copy(
            src_ref=hop,
            dst_ref=panel.at[yh, z].at[PART[1]],
            send_sem=ssem.at[F_ID],
            recv_sem=rsem.at[T_ID + 1],
            device_id=fwd,
            device_id_type=MESH,
        ).start()

    def ring(off):
        return 4 * core + lax.rem(x + turn + off, 4)

    mine, theirs = yh, 1 - yh
    sl, sr, sf = ring(3), ring(1), ring(2)

    def spread(b, k, p):
        u = panel.at[b, s0].at[PART[p]]
        send(u, u, k + p, xright)
        send(u, u, k + 2 + p, xleft)

    def onward(b, k):
        u = panel.at[b, sl].at[PART[0]]
        arrived(u, k)
        send(u, u, k + 4, xright)
        u = panel.at[b, sr].at[PART[1]]
        arrived(u, k + 3)
        send(u, u, k + 5, xleft)

    def beside(b, k, kc):
        u = panel.at[b, sl]
        arrived(u.at[PART[1]], k + 1)
        send(u, u, kc + 1, other)
        u = panel.at[b, sr]
        arrived(u.at[PART[0]], k + 2)
        send(u, u, kc + 2, other)

    def far(b, k, kc):
        u = panel.at[b, sf]
        arrived(u.at[PART[0]], k + 4)
        arrived(u.at[PART[1]], k + 5)
        send(u, u, kc + 3, other)

    def zstep(step):
        got_r = pror.at[yl, lax.rem(z + 8 - step, 8)]
        got_l = pror.at[yl, lax.rem(z + step, 8)]
        arrived(got_r, Z_ID + step - 1)
        arrived(got_l, Z_ID + 4 + step - 1)
        if step < 3:
            send(got_r, got_r, Z_ID + step, zright)
            send(got_l, got_l, Z_ID + 4 + step, zleft)
        else:
            send(got_r.at[PART[0]], got_r.at[PART[0]], Z_ID + 3, zright)
            send(got_l.at[PART[1]], got_l.at[PART[1]], Z_ID + 7, zleft)
        send(got_r, got_r, PY_ID + 2 * step - 1, ynear)
        send(got_l, got_l, PY_ID + 2 * step, ynear)

    u = panel.at[mine, s0]

    @pl.when(own_across)
    def _():
        pltpu.make_async_copy(unit, panel.at[yh, z], lsem.at[0]).wait()

    for p in range(2):
        @pl.when(jnp.logical_not(own_across))
        def _():
            arrived(u.at[PART[p]], T_ID + p)

        send(u.at[PART[p]], u.at[PART[p]], Y_ID + p, yfar)
        spread(mine, X_ID, p)
    send_piece(2)
    send_piece(3)
    send(u, u, CORE_ID, other)
    keep.wait()
    send(unit, zu, Z_ID, zright)
    send(unit, zu, Z_ID + 4, zleft)
    send(zu, zu, PY_ID, ynear)
    build_a(alist, meta, yl, 1)
    onward(mine, X_ID)
    build_a(alist, meta, yl, 2)
    u = panel.at[theirs, s0]
    for p in range(2):
        arrived(u.at[PART[p]], Y_ID + p)
        spread(theirs, X_ID + 6, p)
    send(u, u, CORE_ID + 4, other)
    zstep(1)
    beside(mine, X_ID, CORE_ID)
    build_a(alist, meta, yl, 3)
    onward(theirs, X_ID + 6)
    far(mine, X_ID, CORE_ID)
    zstep(2)
    arrived(mnear, M_ID)
    for n in range(2):
        arrived(anear.at[pl.ds(n * 8, 8)], A_ID + n)
        build_a(anear, mnear, 1 - yl, n)
    beside(theirs, X_ID + 6, CORE_ID + 4)
    far(theirs, X_ID + 6, CORE_ID + 4)
    for n in range(2, 4):
        arrived(anear.at[pl.ds(n * 8, 8)], A_ID + n)
        build_a(anear, mnear, 1 - yl, n)
    for n in range(8):
        s = 4 * (1 - core) + lax.rem(x + turn + (0, 3, 1, 2)[n % 4], 4)
        arrived(panel.at[(mine, theirs)[n // 4], s], CORE_ID + n)

    def build_r(d, at):
        s = lax.rem(z + d, 8)

        def block(b, carry):
            for k in range(8):
                for off, v in zip((0, 32), dense(panel, b, s, k)):
                    hi, lo = split(v)
                    rhi[b, pl.ds(k * 64 + off, 32), pl.ds(at * 128, 128)] = hi
                    rlo[b, pl.ds(k * 64 + off, 32), pl.ds(at * 128, 128)] = lo
            return carry

        lax.fori_loop(0, 2, block, 0)

    left128 = lax.broadcasted_iota(jnp.int32, (128, 128), 1) < 64
    left64 = lax.broadcasted_iota(jnp.int32, (64, 128), 1) < 64

    def chunk(*ds):
        wide = 128 * len(ds)
        for at, d in enumerate(ds):
            build_r(d, at)

        def part(e, carry):
            acc = jnp.zeros((256, wide), F32)
            top = pl.ds(pl.multiple_of(e * 128, 128), 128)
            bot = pl.ds(pl.multiple_of(256 + e * 128, 128), 128)
            for b in range(2):
                h = jnp.concatenate([ahi[b, top, :], ahi[b, bot, :]], axis=0)
                l = jnp.concatenate([alo[b, top, :], alo[b, bot, :]], axis=0)
                rh = rhi[b, :, pl.ds(0, wide)]
                acc = acc + dot(h, rh) + dot(h, rlo[b, :, pl.ds(0, wide)]) + dot(l, rh)
            for at, d in enumerate(ds):
                t, u = acc[:128, at * 128 : at * 128 + 128], acc[128:, at * 128 : at * 128 + 128]
                q[d, e] = jnp.where(left128, t, pltpu.roll(u, 64, 1))
                q[d, 2 + e] = jnp.where(left128, pltpu.roll(t, 64, 1), u)
            return carry

        lax.fori_loop(0, 2, part, 0)

    def rs_id(step, blk, way):
        return RS_ID + (step * 4 + blk) * 2 + way

    def rs_send(d, step, blk, way):
        buf = (rsr, rsl)[way]
        send(q.at[d, blk], buf.at[step, blk], rs_id(step, blk, way), (zright, zleft)[way])

    def rs_add(d, step, blk, way):
        buf = (rsr, rsl)[way]
        arrived(buf.at[step, blk], rs_id(step, blk, way))
        q[d, blk] = q[d, blk] + buf[step, blk]

    def build_t(b, s):
        flag = pror[b, s, pl.ds(256, 8), :]
        for m in range(4):
            parts = []
            for rho in range(8 * m, 8 * m + 8):
                tile = pror[b, s, pl.ds(rho, 8, stride=32), :]
                turned = pltpu.roll(tile, 64, 1)
                parts.append(jnp.where(left8, tile * (1.0 - flag), turned * flag))
                parts.append(jnp.where(left8, turned * (1.0 - flag), tile * flag))
            hi, lo = split(jnp.concatenate(parts, axis=0).T)
            g = b * 8 + s
            rows = pl.ds(pl.multiple_of(g // 8 * 128, 128), 128)
            pthi[lax.rem(g, 2), lax.rem(g // 2, 4), rows, pl.ds(m * 128, 128)] = hi
            ptlo[lax.rem(g, 2), lax.rem(g // 2, 4), rows, pl.ds(m * 128, 128)] = lo

    def own_t(s, carry):
        build_t(yl, s)
        return carry

    def pass_step(step):
        for n in range(4):
            for way, d in ((0, 4 - step), (1, 4 + step)):
                blk = ORDER[way][n]
                if step > 1 or blk % 2 == way:
                    rs_add(d, step - 1, blk, way)
                rs_send(d, step, blk, way)

    zstep(3)
    chunk(4)
    for blk in range(4):
        rs_send(4, 0, blk, blk % 2)
    chunk(3, 5)
    pass_step(1)
    zfar = pror.at[yl, lax.rem(z + 4, 8)]
    arrived(zfar.at[PART[0]], Z_ID + 3)
    arrived(zfar.at[PART[1]], Z_ID + 7)
    send(zfar, zfar, PY_ID + 7, ynear)
    chunk(2, 6)
    lax.fori_loop(0, 8, own_t, 0)
    pass_step(2)
    chunk(1, 7)
    pass_step(3)
    chunk(0)

    near = [z]
    for step in (1, 2, 3):
        near += [lax.rem(z + 8 - step, 8), lax.rem(z + step, 8)]
    near.append(lax.rem(z + 4, 8))
    for n, shard in enumerate(near):
        arrived(pror.at[1 - yl, shard], PY_ID + n)
        build_t(1 - yl, shard)

    def finish(m):
        for e in range(2):
            for way in (0, 1):
                rs_add(0, 3, 2 * m + e, way)
            v = q[0, 2 * m + e]
            hi = v.astype(BF16).astype(F32)
            lo = v - hi
            pcat[m, pl.ds(e * 128, 128), :] = jnp.where(left128, hi, pltpu.roll(lo, 64, 1)).astype(BF16)
            pcat[m, pl.ds(256 + e * 128, 128), :] = jnp.where(left128, pltpu.roll(hi, 64, 1), lo).astype(BF16)

    def coarse_part(gc, gx, m):
        a = dot(pthi[gc, gx], pcat[m])
        v = a + pltpu.roll(a, 64, 1) + dot(ptlo[gc, gx], pcat[m])
        for gy in range(2):
            top, bot = v[gy * 128 : gy * 128 + 64], v[gy * 128 + 64 : gy * 128 + 128]
            cpart[gc, gx, m, gy] = jnp.where(left64, top, pltpu.roll(bot, 64, 1))

    def to_other(gx, m, n):
        coarse_part(1 - core, gx, m)
        send(cpart.at[1 - core, gx, m], crecv.at[gx, m], CC_ID + 4 * m + n, other)

    def from_core(gx, m, n):
        coarse_part(core, gx, m)
        arrived(crecv.at[gx, m], CC_ID + 4 * m + n)
        cpart[core, gx, m] = cpart[core, gx, m] + crecv[gx, m]

    x2 = lax.rem(x + 2, 4)
    xp, xm = lax.rem(x + 1, 4), lax.rem(x + 3, 4)
    cp = cpart.at[core]

    def first(m):
        to_other(x2, m, 0)
        to_other(xp, m, 1)
        from_core(x2, m, 0)
        send(cp.at[x2, m, 0], xr0.at[m], CX_ID + 4 * m, xright)
        send(cp.at[x2, m, 1], xl0.at[m], CX_ID + 4 * m + 1, xleft)

    def sides(m):
        to_other(xm, m, 2)
        from_core(xp, m, 1)
        from_core(xm, m, 2)

    def second(m):
        arrived(xr0.at[m], CX_ID + 4 * m)
        cpart[core, xp, m, 0] = cpart[core, xp, m, 0] + xr0[m]
        send(cp.at[xp, m], xr1.at[m], CX_ID + 4 * m + 2, xright)
        arrived(xl0.at[m], CX_ID + 4 * m + 1)
        cpart[core, xm, m, 1] = cpart[core, xm, m, 1] + xl0[m]
        send(cp.at[xm, m], xl1.at[m], CX_ID + 4 * m + 3, xleft)

    def third(m):
        arrived(xr1.at[m], CX_ID + 4 * m + 2)
        arrived(xl1.at[m], CX_ID + 4 * m + 3)
        cpart[core, x, m, 1 - yh] = cpart[core, x, m, 1 - yh] + xr1[m, 1 - yh] + xl1[m, 1 - yh]
        send(cp.at[x, m, 1 - yh], yrecv.at[m], CY_ID + m, yfar)

    finish(0)
    first(0)
    finish(1)
    first(1)
    sides(0)
    second(0)
    sides(1)
    second(1)
    to_other(x, 0, 3)
    to_other(x, 1, 3)
    from_core(x, 0, 3)
    third(0)
    from_core(x, 1, 3)
    for i in range(8):
        for h in range(2):
            for m in range(2):
                for e in range(2):
                    v = q[0, 2 * m + e, pl.ds(h * 8 + i, 8, stride=16), :]
                    prod_ref[i, m, pl.ds(h * 32 + e * 8, 8), :] = v[:, :64]
                    prod_ref[i, m, pl.ds(h * 32 + 16 + e * 8, 8), :] = v[:, 64:]
    put = pltpu.make_async_copy(prod_ref, prod_hbm, lsem.at[3])
    put.start()
    third(1)
    for m in range(2):
        total = cpart[core, x, m, yh] + xr1[m, yh] + xl1[m, yh]
        arrived(yrecv.at[m], CY_ID + m)
        total = total + yrecv[m]
        coarse_ref[0, m] = total[:, :64]
        coarse_ref[1, m] = total[:, 64:]

    u = panel.at[0, 0]

    @pl.when(jnp.logical_not(own_across))
    def _():
        sent(u.at[PART[0]], T_ID)

    @pl.when(jnp.logical_or(direct, final_hop))
    def _():
        sent(u.at[PART[1]], T_ID + 1)

    @pl.when(first_hop)
    def _():
        sent(hop, H_ID)

    @pl.when(serves)
    def _():
        sent(hop, F_ID)

    zu = pror.at[0, 0]
    for p in range(2):
        part = u.at[PART[p]]

        sent(part, Y_ID + p)
        for k in (X_ID, X_ID + 6):
            sent(part, k + p)
            sent(part, k + 2 + p)
            sent(part, k + 4 + p)
    put.wait()
    sent(meta, M_ID)
    for n in range(4):
        sent(alist.at[pl.ds(0, 8)], A_ID + n)
    for n in range(8):
        sent(u, CORE_ID + n)
        sent(zu, PY_ID + n)
    for n in range(3):
        sent(zu, Z_ID + n)
        sent(zu, Z_ID + 4 + n)
    sent(zu.at[PART[0]], Z_ID + 3)
    sent(zu.at[PART[1]], Z_ID + 7)
    piece = q.at[0, 0]
    for blk in range(4):
        sent(piece, rs_id(0, blk, blk % 2))
        for step in (1, 2, 3):
            for way in (0, 1):
                sent(piece, rs_id(step, blk, way))
    for n in range(8):
        sent(crecv.at[0, 0], CC_ID + n)
    for m in range(2):
        sent(xr0.at[m], CX_ID + 4 * m)
        sent(xl0.at[m], CX_ID + 4 * m + 1)
        sent(xr1.at[m], CX_ID + 4 * m + 2)
        sent(xl1.at[m], CX_ID + 4 * m + 3)
        sent(yrecv.at[m], CY_ID + m)


def shards(op_tiles, op_rows, op_cols, op_count, pro_tiles, pro_cols, pro_live):
    vmem = pl.BlockSpec(memory_space=pltpu.VMEM)
    smem = pl.BlockSpec(memory_space=pltpu.SMEM)
    anywhere = pl.BlockSpec(memory_space=pl.ANY)
    return pl.pallas_call(
        kernel,
        out_shape=(
            jax.ShapeDtypeStruct((8, 2, 64, 64), F32),
            jax.ShapeDtypeStruct((2, 2, 64, 64), F32),
        ),
        in_specs=[anywhere, vmem, vmem, smem, vmem, smem, smem],
        out_specs=(anywhere, vmem),
        scratch_shapes=[
            pltpu.VMEM((LA, 64, 64), F32),
            pltpu.VMEM((8, 2, 64, 64), F32),
            pltpu.VMEM((8, 128), F32),
            pltpu.VMEM((8, 128), F32),
            pltpu.VMEM((UR - UH, 128), F32),
            pltpu.VMEM((UR, 128), F32),
            pltpu.VMEM((32, LA, 128), F32),
            pltpu.VMEM((32, LA, 128), F32),
            pltpu.VMEM((2, 8, UR, 128), F32),
            pltpu.VMEM((2, 8, UR, 128), F32),
            pltpu.VMEM((2, 512, 512), BF16),
            pltpu.VMEM((2, 512, 512), BF16),
            pltpu.VMEM((2, 512, 256), BF16),
            pltpu.VMEM((2, 512, 256), BF16),
            pltpu.VMEM((8, 4, 128, 128), F32),
            pltpu.VMEM((4, 4, 128, 128), F32),
            pltpu.VMEM((4, 4, 128, 128), F32),
            pltpu.VMEM((2, 4, 256, 512), BF16),
            pltpu.VMEM((2, 4, 256, 512), BF16),
            pltpu.VMEM((2, 512, 128), BF16),
            pltpu.VMEM((2, 4, 2, 2, 64, 128), F32),
            pltpu.VMEM((4, 2, 2, 64, 128), F32),
            pltpu.VMEM((2, 64, 128), F32),
            pltpu.VMEM((2, 64, 128), F32),
            pltpu.VMEM((2, 2, 64, 128), F32),
            pltpu.VMEM((2, 2, 64, 128), F32),
            pltpu.VMEM((2, 64, 128), F32),
            pltpu.SemaphoreType.DMA((N_ID,)),
            pltpu.SemaphoreType.DMA((N_ID,)),
            pltpu.SemaphoreType.DMA((4,)),
        ],
        compiler_params=pltpu.CompilerParams(
            collective_id=0, has_side_effects=True, vmem_limit_bytes=60 * 1024 * 1024
        ),
    )(
        op_tiles.reshape(32, 64, 64), op_rows.T, op_cols.T, op_count,
        pro_tiles.reshape(8, 64, 64), pro_cols.T, pro_live.T,
    )


def solution(mesh):
    return jax.shard_map(
        shards,
        mesh=mesh,
        in_specs=(
            P("row", "col", None, None),
            P("row", "col"),
            P("row", "col"),
            P("row", "col"),
            P("row", "col", None, None),
            P("row", "col"),
            P("row", "col"),
        ),
        out_specs=(P("row", "col", None, None), P("row", "col", None, None)),
        check_vma=False,
    )
```
